128 devices in a mesh: seq: 16 (over z, x), inner: 8 (over y, core).
Axes of the slice: x: 4, y: 4, z: 4, core: 2. Of those that a mesh axis runs over, the one named last changes fastest.
Arguments:
- log_mel: bfloat16 [114688, 320], P(('seq', 'inner')), may hold values from -6 to 6
- lengths: int32 [128, 4], replicated, may hold values from 1 to 893, as said below
- first_kernel: bfloat16 [9, 128], replicated, may hold values from -2 to 2
- first_bias: float32 [128], replicated, may hold values from -3 to 3
- second_kernel: bfloat16 [1152, 128], replicated, may hold values from -0.1875 to 0.1875
- second_bias: float32 [128], replicated, may hold values from -3 to 3
- embed_weight: bfloat16 [2560, 1024], replicated, may hold values from -0.125 to 0.125
- norm_gain: float32 [1024], replicated, may hold values from 0.1 to 1.9
- head_weight: bfloat16 [1024, 3072], replicated
- output_weight: bfloat16 [1024, 1024], replicated, may hold values from -0.1875 to 0.1875
Outputs:
- encoded: bfloat16 [65536, 1024], P(('seq', 'inner'))
The draws below stay inside these ranges and needn't reach their ends.
Inputs may be any that keep to these rules, and one draw needn't show every extreme that they name: `lengths`: every length is 1 or more. The frames of owner d begin at d * 512 + e_d with e_d between -192 and 192; e_0 = 0, the frames of all owners together are exactly 65536, and in every draw some owner has e_d = 192 and another e_d = -192. In every draw some utterance has exactly 893 frames.
All inputs are finite; a program needn't handle non-finite values.
Results may differ from the reference program's by a relative error of at most 0.008.
The reference program's roundings to bfloat16 on the way count: a program that leaves them out, or rounds other values in their place, can miss the bound.
Values may be sent and summed in bfloat16 or wider, within the bound.
A program may use at most 256 MiB of HBM per device.

```python
import jax
import jax.numpy as jnp
from jax import lax

MEL = 80
CH = 128
D = 1024
HEADS = 16
SPAN = 64
LEFT_SPANS = 4
CTX = 320
SHARD = 512
MARGIN = 192
CAP = 896
UTT_DEV = 4
FRAMES = 65536
DEVICES = 128


def draw_lengths(key, part):
    key_drift, key_pick, key_share = jax.random.split(jax.random.fold_in(key, 11), 3)
    owners = DEVICES
    drift = jax.random.randint(key_drift, (owners + 1,), -MARGIN, MARGIN + 1)
    picked = jax.random.randint(key_pick, (), 1, owners - 1)
    places = jnp.arange(owners + 1)
    drift = jnp.where(places == picked, -MARGIN, drift)
    drift = jnp.where(places == picked + 1, MARGIN, drift)
    drift = jnp.where((places == 0) | (places == owners), 0, drift)
    counts = SHARD + drift[1:] - drift[:-1]
    shares = jax.random.randint(key_share, (owners, UTT_DEV), 1, 5)
    totals = jnp.sum(shares, axis=1, keepdims=True)
    edges = counts[:, None] * jnp.cumsum(shares, axis=1) // totals
    lower_edges = jnp.concatenate([jnp.zeros((owners, 1), edges.dtype), edges[:, :-1]], axis=1)
    split = edges - lower_edges
    columns = jnp.arange(UTT_DEV)
    forced = jnp.where(columns == UTT_DEV - 1, CAP - UTT_DEV + 1, 1)
    rows = jnp.arange(owners)
    result = jnp.where((rows == picked)[:, None], forced[None, :], split)
    return result.astype(jnp.int32)


def draw_head_weight(key, part):
    key_base = jax.random.fold_in(jax.random.fold_in(key, 7), 0)
    return (jax.random.normal(key_base, (D, 3 * D), jnp.float32) * D ** (-0.5)).astype(jnp.bfloat16)


def block_levels(own_key, shape, cuts, low, top_value):
    def one(dim, shards_of):
        draws = jax.random.uniform(jax.random.fold_in(jax.random.fold_in(own_key, 6), dim), (shards_of,), jnp.float32, low / len(cuts), top_value / len(cuts))
        return jnp.repeat(jnp.exp(draws), shape[dim] // shards_of).reshape((-1,) + (1,) * (len(shape) - dim - 1))

    level = one(*cuts[0])
    for cut in cuts[1:]:
        level = level * one(*cut)
    return level


def noise(own_key, dims, scale, bound, shards=(), held_as=jnp.bfloat16):
    values = scale * jax.random.normal(own_key, dims, jnp.float32)
    if shards:
        values = values * block_levels(own_key, dims, shards, -0.22, 0.18)
    return jnp.clip(values, -bound, bound).astype(held_as)


def setup_inputs(seed: int = 0) -> dict:
    arg_keys = jax.random.split(jax.random.key(seed), 11)
    log_mel = noise(arg_keys[0], (DEVICES * CAP, 4 * MEL), 1.0, 6.0, ((0, 128),))
    lengths = draw_lengths(jax.random.fold_in(arg_keys[10], 71), 0)
    first_kernel = noise(arg_keys[2], (9, CH), 9 ** -0.5, 2.0)
    first_bias = noise(arg_keys[3], (CH,), 0.5, 3.0, (), jnp.float32)
    second_kernel = noise(arg_keys[4], (9 * CH, CH), (9 * CH) ** -0.5, 0.1875)
    second_bias = noise(arg_keys[5], (CH,), 0.5, 3.0, (), jnp.float32)
    embed_weight = noise(arg_keys[6], ((MEL // 4) * CH, D), ((MEL // 4) * CH) ** -0.5, 0.125)
    norm_gain = jnp.clip(1.0 + 0.18 * jax.random.normal(arg_keys[7], (D,), jnp.float32), 0.1, 1.9)
    head_weight = draw_head_weight(jax.random.fold_in(arg_keys[10], 71), 0)
    output_weight = noise(arg_keys[9], (D, D), D ** -0.5, 0.1875)
    return dict(log_mel=log_mel, lengths=lengths, first_kernel=first_kernel, first_bias=first_bias, second_kernel=second_kernel, second_bias=second_bias, embed_weight=embed_weight, norm_gain=norm_gain, head_weight=head_weight, output_weight=output_weight)


def front_end(raw_rows, seg_ids, first_kernel, first_bias, second_kernel, second_bias, embed_weight):
    row_count = raw_rows.shape[0] - 1
    mel_bins = raw_rows.shape[1] // 4
    usable = seg_ids >= 0
    joined = jnp.concatenate([jnp.zeros((1,), bool), (seg_ids[1:] == seg_ids[:-1]) & usable[1:]])
    frames = jnp.where(usable[:, None], raw_rows, jnp.zeros_like(raw_rows)).reshape(row_count + 1, 4, mel_bins)
    shifted = jnp.concatenate([jnp.zeros((1, mel_bins), raw_rows.dtype), frames[:-1, 3]], axis=0)
    before = jnp.where(joined[:, None], shifted, jnp.zeros_like(shifted))
    even_taps = jnp.stack([before, frames[:, 0], frames[:, 1]], axis=1)
    odd_taps = jnp.stack([frames[:, 1], frames[:, 2], frames[:, 3]], axis=1)
    time_taps = jnp.stack([even_taps, odd_taps], axis=1)
    padded = jnp.pad(time_taps, ((0, 0), (0, 0), (0, 0), (1, 0)))
    freq_taps = jnp.stack([padded[..., 0:mel_bins:2], padded[..., 1:mel_bins + 1:2], padded[..., 2:mel_bins + 2:2]], axis=-1)
    patches = jnp.transpose(freq_taps, (0, 1, 3, 2, 4)).reshape(-1, 9)
    first_out = jnp.dot(patches, first_kernel, preferred_element_type=jnp.float32) + first_bias
    first_out = jnp.maximum(first_out, 0.0).astype(jnp.bfloat16).reshape(row_count + 1, 2, mel_bins // 2, -1)
    channels = first_out.shape[-1]
    earlier = jnp.where(joined[1:, None, None], first_out[:-1, 1], jnp.zeros_like(first_out[:-1, 1]))
    second_in = jnp.stack([earlier, first_out[1:, 0], first_out[1:, 1]], axis=1)
    half_bins = mel_bins // 2
    spread = jnp.pad(second_in, ((0, 0), (0, 0), (1, 0), (0, 0)))
    summed = jnp.zeros((row_count * (half_bins // 2), second_kernel.shape[1]), jnp.float32)
    for tap_time in range(3):
        for tap_freq in range(3):
            slab_rows = spread[:, tap_time, tap_freq:tap_freq + half_bins:2].reshape(-1, channels)
            offset = (tap_time * 3 + tap_freq) * channels
            summed = summed + jnp.dot(slab_rows, second_kernel[offset:offset + channels], preferred_element_type=jnp.float32)
    second_out = jnp.maximum(summed + second_bias, 0.0).astype(jnp.bfloat16).reshape(row_count, -1)
    return jnp.dot(second_out, embed_weight, preferred_element_type=jnp.float32).astype(jnp.bfloat16)

def positions(spots, starts, frame_total):
    usable = (spots >= 0) & (spots < frame_total)
    reached = starts[None, :] <= spots[:, None]
    seg_ids = lax.optimization_barrier(jnp.sum(reached.astype(jnp.int32), axis=1)).astype(jnp.int32) - 1
    begins = lax.optimization_barrier(jnp.max(jnp.where(reached, starts[None, :], jnp.zeros_like(starts[None, :])), axis=1))
    seg_ids = jnp.where(usable, seg_ids, -1).astype(jnp.int32)
    return (seg_ids, (spots - begins).astype(jnp.int32))

def visible(query_seg, query_pos, key_seg, key_pos):
    query_span = query_pos // SPAN
    key_span = key_pos // SPAN
    same_utt = (query_seg[:, None] == key_seg[None, :]) & (key_seg[None, :] >= 0)
    return same_utt & (key_span[None, :] >= query_span[:, None] - LEFT_SPANS) & (key_span[None, :] <= query_span[:, None])

def layer_norm(rows_in, gain):
    values = rows_in.astype(jnp.float32)
    center = values - lax.optimization_barrier(jnp.mean(values, axis=1, keepdims=True))
    spread = lax.optimization_barrier(jnp.mean(center * center, axis=1, keepdims=True))
    return (center * lax.rsqrt(spread + 1e-05) * gain).astype(jnp.bfloat16)

def attend(queries, keys, values, allowed):
    head_size = queries.shape[1] // HEADS
    query_heads = queries.astype(jnp.float32).reshape(-1, HEADS, head_size)
    key_heads = keys.astype(jnp.float32).reshape(-1, HEADS, head_size)
    value_heads = values.astype(jnp.float32).reshape(-1, HEADS, head_size)
    scores = jnp.einsum('qhd,khd->hqk', query_heads, key_heads) * head_size ** (-0.5)
    scores = jnp.where(allowed[None], scores, jnp.float32(-1e+30))
    peak = lax.optimization_barrier(jnp.max(scores, axis=-1, keepdims=True))
    expd = jnp.exp(scores - peak)
    probs = (expd / lax.optimization_barrier(jnp.sum(expd, axis=-1, keepdims=True))).astype(jnp.bfloat16)
    mixed = jnp.einsum('hqk,khd->qhd', probs.astype(jnp.float32), value_heads)
    return mixed.reshape(queries.shape[0], -1).astype(jnp.bfloat16)

def reference(log_mel, lengths, first_kernel, first_bias, second_kernel, second_bias, embed_weight, norm_gain, head_weight, output_weight):
    owners = lengths.shape[0]
    flat = lengths.reshape(-1).astype(jnp.int32)
    starts = (jnp.cumsum(flat) - flat).astype(jnp.int32)
    owner_len = lax.optimization_barrier(jnp.sum(lengths, axis=1)).astype(jnp.int32)
    owner_start = (jnp.cumsum(owner_len) - owner_len).astype(jnp.int32)
    spots = jnp.arange(FRAMES, dtype=jnp.int32)
    owner_of = (lax.optimization_barrier(jnp.sum((owner_start[None, :] <= spots[:, None]).astype(jnp.int32), axis=1)) - 1).astype(jnp.int32)
    source = (owner_of * CAP + spots - owner_of * SHARD + MARGIN).astype(jnp.int32)
    raw_global = jnp.take(log_mel, source, axis=0)
    raw_padded = jnp.concatenate([jnp.zeros((1, log_mel.shape[1]), log_mel.dtype), raw_global], axis=0)

    def front_block(index):
        begin = (index * SHARD).astype(jnp.int32)
        window = lax.dynamic_slice_in_dim(raw_padded, begin, SHARD + 1, 0)
        seg_ids, unused_pos = positions(begin - 1 + jnp.arange(SHARD + 1, dtype=jnp.int32), starts, FRAMES)
        return front_end(window, seg_ids, first_kernel, first_bias, second_kernel, second_bias, embed_weight)
    block_ids = jnp.arange(owners, dtype=jnp.int32)
    embedded = lax.map(front_block, block_ids).reshape(FRAMES, -1)
    normed = layer_norm(embedded, norm_gain)
    packed = jnp.dot(normed, head_weight, preferred_element_type=jnp.float32).astype(jnp.bfloat16)
    width = normed.shape[1]
    key_vals = packed[:, width:]
    kv_padded = jnp.concatenate([jnp.zeros((CTX, 2 * width), jnp.bfloat16), key_vals, jnp.zeros((SPAN, 2 * width), jnp.bfloat16)], axis=0)
    key_rows = CTX + SHARD + SPAN

    def attend_block(index):
        begin = (index * SHARD).astype(jnp.int32)
        queries = lax.dynamic_slice_in_dim(packed, begin, SHARD, 0)[:, :width]
        context = lax.dynamic_slice_in_dim(kv_padded, begin, key_rows, 0)
        query_seg, query_pos = positions(begin + jnp.arange(SHARD, dtype=jnp.int32), starts, FRAMES)
        key_seg, key_pos = positions(begin - CTX + jnp.arange(key_rows, dtype=jnp.int32), starts, FRAMES)
        allowed = visible(query_seg, query_pos, key_seg, key_pos)
        mixed = attend(queries, context[:, :width], context[:, width:], allowed)
        residual = lax.dynamic_slice_in_dim(embedded, begin, SHARD, 0)
        output = residual.astype(jnp.float32) + jnp.dot(mixed, output_weight, preferred_element_type=jnp.float32)
        return output.astype(jnp.bfloat16)
    return lax.map(attend_block, block_ids).reshape(FRAMES, -1)
```

```python
import functools

import jax
import jax.numpy as jnp
from jax import lax
from jax.experimental import pallas as pl
from jax.experimental.pallas import tpu as pltpu
from jax.sharding import PartitionSpec as P

HEADS = 16
SPAN = 64
LEFT_SPANS = 4
CTX = 320
SHARD = 512
MARGIN = 192
MEL = 80
CH = 128
D = 1024
BINS = 20
PAD = 16
LOW_ROWS = MARGIN + PAD
AXES = ("seq", "inner")
F32 = jnp.float32
BF16 = jnp.bfloat16


def bounds(device, devices, lens_ref, lens_smem):
    rows = lax.broadcasted_iota(jnp.int32, lens_ref.shape, 0)
    before = jnp.where(rows < device - 1, lens_ref[...].astype(F32), 0.0)
    base = jnp.sum(jnp.sum(before, axis=0, keepdims=True), axis=1, keepdims=True).astype(jnp.int32)
    starts = []
    total = jnp.int32(0)
    for step in (-1, 0, 1):
        owner = device + step
        real = (owner >= 0) & (owner < devices)
        safe = jnp.clip(owner, 0, devices - 1)
        for column in range(lens_smem.shape[1]):
            starts.append(total)
            total = total + jnp.where(real, lens_smem[safe, column], 0)
    return base, starts


def locate(spots, base, starts):
    rel = spots - base
    seg = jnp.zeros_like(rel)
    begin = jnp.zeros_like(rel)
    for start in starts[1:]:
        reached = rel >= start
        seg = seg + reached.astype(jnp.int32)
        begin = jnp.where(reached, start, begin)
    return seg, rel - begin


def codes(seg, pos):
    return seg * 64 + lax.shift_right_arithmetic(pos, 6)


def build_taps(first_kernel, first_bias, kext):
    kext[...] = jnp.zeros_like(kext)
    taps = first_kernel[...].astype(F32)
    for a in range(3):
        for b in range(3):
            row = taps[3 * a + b : 3 * a + b + 1, :]
            kext[5 * a + b : 5 * a + b + 1, 0:CH] = row
            kext[5 * a + b + 2 : 5 * a + b + 3, CH : 2 * CH] = row
    rest = first_bias[...]
    for part in range(3):
        piece = rest.astype(BF16).astype(F32)
        rest = rest - piece
        kext[15 + part : 16 + part, 0:CH] = piece
        kext[15 + part : 16 + part, CH : 2 * CH] = piece


def build_first(kext, w1):
    row = lax.broadcasted_iota(jnp.int32, (256, 32), 0)
    col = lax.broadcasted_iota(jnp.int32, (256, 32), 1)
    tap = (row >= MEL).astype(jnp.int32) + (row >= 2 * MEL).astype(jnp.int32)
    mel = row - MEL * tap
    wide = kext[...].astype(BF16)

    def body(f, carry):
        off = mel - 4 * f + 1
        inside = (off >= 0) & (off <= 4) & (row < 3 * MEL)
        want = jnp.where(inside, 5 * tap + off, jnp.where(row >= 3 * MEL, row - 3 * MEL + 15, -1))
        select = jnp.where(col == want, 1.0, 0.0).astype(BF16)
        block = jnp.dot(select, wide, preferred_element_type=F32)
        w1[:, pl.ds(pl.multiple_of(f * 256, 256), 256)] = block.astype(BF16)
        return carry

    lax.fori_loop(0, BINS, body, 0, unroll=2)


def build_second(second_kernel, w2):
    for a in range(3):
        base = 3 * a * CH
        w2[256 * a : 256 * a + 256, 0:CH] = second_kernel[base + CH : base + 3 * CH, :]
        w2[256 * a : 256 * a + CH, CH : 2 * CH] = jnp.zeros((CH, CH), BF16)
        w2[256 * a + CH : 256 * a + 256, CH : 2 * CH] = second_kernel[base : base + CH, :]


def build_inputs(device, base, starts, raw, low, high, rows32, x):
    count = SHARD + PAD
    spots = device * SHARD - PAD + lax.broadcasted_iota(jnp.int32, (count, 1), 0)
    seg, pos = locate(spots, base, starts)
    owner = lax.shift_right_arithmetic(seg, 2)
    first = MARGIN - PAD
    rows32[0:LOW_ROWS, :] = jnp.where(
        owner[0:LOW_ROWS] == 0, low[...].astype(F32), raw[first : first + LOW_ROWS, :].astype(F32)
    )
    rows32[LOW_ROWS : count - MARGIN, :] = raw[first + LOW_ROWS : first + count - MARGIN, :].astype(F32)
    rows32[count - MARGIN : count, :] = jnp.where(
        owner[count - MARGIN :] == 2,
        high[...].astype(F32),
        raw[first + count - MARGIN : first + count, :].astype(F32),
    )
    joined = pos[PAD:] > 0
    now = rows32[PAD:count, :]
    before = jnp.where(joined, rows32[PAD - 1 : count - 1, :], 0.0)
    ones = jnp.ones((SHARD, 16), F32)
    kept = jnp.where(joined, ones, 0.0)
    x[0:SHARD, :] = jnp.concatenate([before[:, MEL:], kept], axis=1).astype(BF16)
    x[SHARD : 2 * SHARD, :] = jnp.concatenate(
        [before[:, 3 * MEL :], now[:, : 2 * MEL], ones], axis=1
    ).astype(BF16)
    x[2 * SHARD :, :] = jnp.concatenate([now[:, MEL:], ones], axis=1).astype(BF16)


def convolve(x, w1, w2, second_bias, ycat, lower, second_out):
    lower[...] = jnp.zeros_like(lower)
    bias = second_bias[...]

    def body(f, carry):
        block = w1[:, pl.ds(pl.multiple_of(f * 256, 256), 256)]
        for a in range(3):
            y = jnp.dot(x[a * SHARD : (a + 1) * SHARD, :], block, preferred_element_type=F32)
            ycat[:, 256 * a : 256 * a + 256] = jnp.maximum(y, 0.0).astype(BF16)
        r = jnp.dot(ycat[...], w2[...], preferred_element_type=F32)
        out = jnp.maximum(r[:, :CH] + lower[...] + bias, 0.0).astype(BF16)
        lower[...] = r[:, CH:]
        second_out[:, pl.ds(pl.multiple_of(f * CH, CH), CH)] = out
        return carry

    lax.fori_loop(0, BINS, body, 0)


def front_kernel(
    raw,
    low,
    high,
    lens_ref,
    lens_smem,
    first_kernel,
    first_bias,
    second_kernel,
    second_bias,
    gain,
    embed_hbm,
    head_hbm,
    embedded,
    normed,
    packed,
    kext,
    w1,
    w2,
    rows32,
    x,
    ycat,
    lower,
    second_out,
    embed_w,
    head_w,
    sems,
):
    load_embed = pltpu.make_async_copy(embed_hbm, embed_w, sems.at[0])
    load_head = pltpu.make_async_copy(head_hbm, head_w, sems.at[1])
    load_embed.start()
    load_head.start()
    device = lax.axis_index(AXES)
    devices = lax.axis_size(AXES)
    base, starts = bounds(device, devices, lens_ref, lens_smem)
    build_taps(first_kernel, first_bias, kext)
    build_first(kext, w1)
    build_second(second_kernel, w2)
    build_inputs(device, base, starts, raw, low, high, rows32, x)
    convolve(x, w1, w2, second_bias, ycat, lower, second_out)
    load_embed.wait()

    def embed_step(n, carry):
        cols = pl.ds(pl.multiple_of(n * 256, 256), 256)
        embedded[:, cols] = jnp.dot(
            second_out[...], embed_w[:, cols], preferred_element_type=F32
        ).astype(BF16)
        return carry

    lax.fori_loop(0, D // 256, embed_step, 0)

    def norm_step(r, carry):
        rows = pl.ds(pl.multiple_of(r * 64, 64), 64)
        values = embedded[rows, :].astype(F32)
        center = values - jnp.mean(values, axis=1, keepdims=True)
        spread = jnp.mean(center * center, axis=1, keepdims=True)
        normed[rows, :] = (center * lax.rsqrt(spread + 1e-05) * gain[...]).astype(BF16)
        return carry

    lax.fori_loop(0, SHARD // 64, norm_step, 0)
    load_head.wait()

    def head_step(n, carry):
        cols = pl.ds(pl.multiple_of(n * 256, 256), 256)
        packed[:, cols] = jnp.dot(
            normed[...], head_w[:, cols], preferred_element_type=F32
        ).astype(BF16)
        return carry

    lax.fori_loop(0, 3 * D // 256, head_step, 0)


def attend_kernel(
    packed,
    embedded,
    before,
    after,
    lens_ref,
    lens_smem,
    head_hbm,
    out_hbm,
    encoded,
    keys,
    vals,
    mixed,
    hide,
    head_w,
    out_w,
    sems,
):
    load_head = pltpu.make_async_copy(head_hbm.at[:, D:], head_w, sems.at[0])
    load_out = pltpu.make_async_copy(out_hbm, out_w, sems.at[1])
    load_head.start()
    load_out.start()
    device = lax.axis_index(AXES)
    devices = lax.axis_size(AXES)
    base, starts = bounds(device, devices, lens_ref, lens_smem)
    key_rows = CTX + SHARD + SPAN
    keys[CTX : CTX + SHARD, :] = packed[:, D : 2 * D]
    vals[CTX : CTX + SHARD, :] = packed[:, 2 * D :]
    spots = device * SHARD - CTX + lax.broadcasted_iota(jnp.int32, (1, key_rows), 1)
    key_code = codes(*locate(spots, base, starts))
    key_code = jnp.where((spots >= 0) & (spots < devices * SHARD), key_code, -1000)
    for block in range(4):
        q_spots = device * SHARD + block * 128 + lax.broadcasted_iota(jnp.int32, (128, 1), 0)
        q_code = codes(*locate(q_spots, base, starts))
        gap = q_code - key_code[:, block * 128 : block * 128 + 512]
        hide[block] = jnp.where((gap >= 0) & (gap <= LEFT_SPANS), 0.0, -1e30)
    load_head.wait()

    def context_step(n, carry):
        cols = pl.ds(pl.multiple_of(n * 256, 256), 256)
        for src, width in ((0, keys), (D, vals)):
            block = head_w[:, pl.ds(pl.multiple_of(n * 256 + src, 256), 256)]
            width[0:CTX, cols] = jnp.dot(before[...], block, preferred_element_type=F32).astype(BF16)
            width[CTX + SHARD :, cols] = jnp.dot(
                after[...], block, preferred_element_type=F32
            ).astype(BF16)
        return carry

    lax.fori_loop(0, D // 256, context_step, 0)
    left = lax.broadcasted_iota(jnp.int32, (128, CH), 1) < 64
    ones = jnp.ones((512, CH), BF16)

    def head_step(step, carry):
        block = step // 8
        pair = step - block * 8
        cols = pl.ds(pl.multiple_of(pair * CH, CH), CH)
        q_rows = pl.ds(pl.multiple_of(block * 128, 128), 128)
        k_rows = pl.ds(pl.multiple_of(block * 128, 128), 512)
        q = packed[q_rows, cols] * BF16(0.125)
        k = keys[k_rows, cols]
        v = jnp.concatenate([vals[k_rows, cols], ones], axis=1)
        outs = []
        for half in (left, jnp.logical_not(left)):
            s = lax.dot_general(
                jnp.where(half, q, BF16(0)),
                k,
                (((1,), (1,)), ((), ())),
                preferred_element_type=F32,
            )
            s = s + hide[block]
            p = jnp.exp(s - jnp.max(s, axis=1, keepdims=True)).astype(BF16)
            o = jnp.dot(p, v, preferred_element_type=F32)
            outs.append(o[:, :CH] / o[:, CH:])
        mixed[q_rows, cols] = jnp.where(left, outs[0], outs[1]).astype(BF16)
        return carry

    lax.fori_loop(0, 32, head_step, 0)
    load_out.wait()

    def out_step(n, carry):
        cols = pl.ds(pl.multiple_of(n * 256, 256), 256)
        total = embedded[:, cols].astype(F32) + jnp.dot(
            mixed[...], out_w[:, cols], preferred_element_type=F32
        )
        encoded[:, cols] = total.astype(BF16)
        return carry

    lax.fori_loop(0, D // 256, out_step, 0)


VMEM = pl.BlockSpec(memory_space=pltpu.VMEM)
SMEM = pl.BlockSpec(memory_space=pltpu.SMEM)
HBM = pl.BlockSpec(memory_space=pl.ANY)


def front(raw, low, high, lengths, first_kernel, first_bias, second_kernel, second_bias, gain, embed_w, head_w):
    return pl.pallas_call(
        front_kernel,
        out_shape=[
            jax.ShapeDtypeStruct((SHARD, D), BF16),
            jax.ShapeDtypeStruct((SHARD, D), BF16),
            jax.ShapeDtypeStruct((SHARD, 3 * D), BF16),
        ],
        in_specs=[VMEM, VMEM, VMEM, VMEM, SMEM, VMEM, VMEM, VMEM, VMEM, VMEM, HBM, HBM],
        out_specs=[VMEM] * 3,
        scratch_shapes=[
            pltpu.VMEM((32, 256), F32),
            pltpu.VMEM((256, BINS * 256), BF16),
            pltpu.VMEM((768, 256), BF16),
            pltpu.VMEM((SHARD + PAD, 4 * MEL), F32),
            pltpu.VMEM((3 * SHARD, 256), BF16),
            pltpu.VMEM((SHARD, 768), BF16),
            pltpu.VMEM((SHARD, CH), F32),
            pltpu.VMEM((SHARD, BINS * CH), BF16),
            pltpu.VMEM(embed_w.shape, BF16),
            pltpu.VMEM(head_w.shape, BF16),
            pltpu.SemaphoreType.DMA((2,)),
        ],
        compiler_params=pltpu.CompilerParams(vmem_limit_bytes=56 * 2**20),
        name="front",
    )(raw, low, high, lengths, lengths, first_kernel, first_bias, second_kernel, second_bias, gain, embed_w, head_w)


def attention(packed, embedded, before, after, lengths, head_w, out_w):
    key_rows = CTX + SHARD + SPAN
    return pl.pallas_call(
        attend_kernel,
        out_shape=jax.ShapeDtypeStruct((SHARD, D), BF16),
        in_specs=[VMEM, VMEM, VMEM, VMEM, VMEM, SMEM, HBM, HBM],
        out_specs=VMEM,
        scratch_shapes=[
            pltpu.VMEM((key_rows, D), BF16),
            pltpu.VMEM((key_rows, D), BF16),
            pltpu.VMEM((SHARD, D), BF16),
            pltpu.VMEM((4, 128, 512), F32),
            pltpu.VMEM((D, 2 * D), BF16),
            pltpu.VMEM((D, D), BF16),
            pltpu.SemaphoreType.DMA((2,)),
        ],
        compiler_params=pltpu.CompilerParams(vmem_limit_bytes=56 * 2**20),
        name="attend",
    )(packed, embedded, before, after, lengths, lengths, head_w, out_w)


def shifted(value, by):
    size = lax.axis_size(AXES)
    pairs = [(i, i + by) for i in range(size) if 0 <= i + by < size]
    return lax.ppermute(value, AXES, pairs)


def on_device(
    log_mel,
    lengths,
    first_kernel,
    first_bias,
    second_kernel,
    second_bias,
    embed_weight,
    norm_gain,
    head_weight,
    output_weight,
):
    cap = log_mel.shape[0]
    low = shifted(log_mel[cap - LOW_ROWS :], 1)
    high = shifted(log_mel[:MARGIN], -1)
    embedded, normed, packed = front(
        log_mel,
        low,
        high,
        lengths,
        first_kernel,
        first_bias.reshape(1, -1),
        second_kernel,
        second_bias.reshape(1, -1),
        norm_gain.reshape(1, -1),
        embed_weight,
        head_weight,
    )
    before = shifted(normed[SHARD - CTX :], 1)
    after = shifted(normed[:SPAN], -1)
    return attention(packed, embedded, before, after, lengths, head_weight, output_weight)


def solution(mesh):
    return jax.shard_map(
        on_device,
        mesh=mesh,
        in_specs=(P(AXES, None), P(), P(), P(), P(), P(), P(), P(), P(), P()),
        out_specs=P(AXES, None),
        check_vma=False,
    )
```

```python
import jax
import jax.numpy as jnp
from jax import lax
from jax.experimental import pallas as pl
from jax.experimental.pallas import tpu as pltpu
from jax.sharding import PartitionSpec as P

SPAN = 64
LEFT_SPANS = 4
CTX = 320
SHARD = 512
MARGIN = 192
MEL = 80
CH = 128
D = 1024
BINS = 20
CUT = 192
WIDE = 640
SIDE = 256
QB = 128
QK = 512
KEY_ROWS = CTX + SHARD + SPAN
AXES = ("seq", "inner")
F32 = jnp.float32
BF16 = jnp.bfloat16
MESH = pl.DeviceIdType.MESH


def bounds(device, devices, lens_ref, lens_smem):
    owners = lax.broadcasted_iota(jnp.int32, lens_ref.shape, 1)
    before = jnp.where(owners < device - 1, lens_ref[...].astype(F32), 0.0)
    base = jnp.sum(jnp.sum(before, axis=0, keepdims=True), axis=1, keepdims=True).astype(jnp.int32)
    starts = []
    total = jnp.int32(0)
    for step in (-1, 0, 1):
        owner = device + step
        real = (owner >= 0) & (owner < devices)
        safe = lax.rem(owner + devices, devices)
        for column in range(lens_smem.shape[0]):
            starts.append(total)
            total = total + jnp.where(real, lens_smem[column, safe], 0)
    return base, starts


def locate(spots, base, starts):
    rel = spots - base
    seg = jnp.zeros_like(rel)
    begin = jnp.zeros_like(rel)
    for start in starts[1:]:
        reached = rel >= start
        seg = seg + reached.astype(jnp.int32)
        begin = jnp.where(reached, start, begin)
    return seg, rel - begin


def codes(seg, pos):
    return seg * 64 + lax.shift_right_arithmetic(pos, 6)


def build_taps(first_kernel, first_bias, kext):
    kext[...] = jnp.zeros_like(kext)
    taps = first_kernel[...].astype(F32)
    for a in range(3):
        for b in range(3):
            row = taps[3 * a + b : 3 * a + b + 1, :]
            kext[5 * a + b : 5 * a + b + 1, 0:CH] = row
            kext[5 * a + b + 2 : 5 * a + b + 3, CH : 2 * CH] = row
    rest = first_bias[...]
    for part in range(3):
        piece = rest.astype(BF16).astype(F32)
        rest = rest - piece
        kext[15 + part : 16 + part, 0:CH] = piece
        kext[15 + part : 16 + part, CH : 2 * CH] = piece


def build_first(kext, w1):
    row = lax.broadcasted_iota(jnp.int32, (256, 32), 0)
    col = lax.broadcasted_iota(jnp.int32, (256, 32), 1)
    tap = (row >= MEL).astype(jnp.int32) + (row >= 2 * MEL).astype(jnp.int32)
    mel = row - MEL * tap
    wide = kext[...].astype(BF16)

    def body(f, carry):
        off = mel - 4 * f + 1
        inside = (off >= 0) & (off <= 4) & (row < 3 * MEL)
        want = jnp.where(inside, 5 * tap + off, jnp.where(row >= 3 * MEL, row - 3 * MEL + 15, -1))
        select = jnp.where(col == want, 1.0, 0.0).astype(BF16)
        block = jnp.dot(select, wide, preferred_element_type=F32)
        w1[:, pl.ds(pl.multiple_of(f * 256, 256), 256)] = block.astype(BF16)
        return carry

    lax.fori_loop(0, BINS, body, 0, unroll=4)


def build_second(second_kernel, w2):
    for a in range(3):
        base = 3 * a * CH
        w2[256 * a : 256 * a + 256, 0:CH] = second_kernel[base + CH : base + 3 * CH, :]
        w2[256 * a : 256 * a + CH, CH : 2 * CH] = jnp.zeros((CH, CH), BF16)
        w2[256 * a + CH : 256 * a + 256, CH : 2 * CH] = second_kernel[base : base + CH, :]


def select_rows(device, base, starts, raw, low, high, rows32):
    spots = device * SHARD - 64 + lax.broadcasted_iota(jnp.int32, (1, WIDE), 1)
    seg, unused_pos = locate(spots, base, starts)
    owner = lax.shift_right_arithmetic(seg, 2)
    parts = [
        jnp.where(owner[:, :SIDE] == 0, low[...].astype(F32), raw[:, 128:384].astype(F32)),
        raw[:, 384:512].astype(F32),
        jnp.where(owner[:, WIDE - SIDE :] == 2, high[...].astype(F32), raw[:, 512:768].astype(F32)),
    ]
    rows32[...] = jnp.concatenate(parts, axis=1).T


def build_inputs(begin, count, joined, rows32, x):
    here = joined[begin : begin + count]
    now = rows32[64 + begin : 64 + begin + count, :]
    before = jnp.where(here, rows32[63 + begin : 63 + begin + count, :], 0.0)
    ones = jnp.ones((count, 16), F32)
    kept = jnp.where(here, ones, 0.0)
    x[0:count, :] = jnp.concatenate([before[:, MEL:], kept], axis=1).astype(BF16)
    x[count : 2 * count, :] = jnp.concatenate(
        [before[:, 3 * MEL :], now[:, : 2 * MEL], ones], axis=1
    ).astype(BF16)
    x[2 * count :, :] = jnp.concatenate([now[:, MEL:], ones], axis=1).astype(BF16)


def convolve(count, x, w1, w2, second_bias, ycat, lower, second_out):
    bias = second_bias[...]
    lower[0, 0:count, :] = jnp.zeros((count, CH), F32)

    def body(step, carry):
        for u in range(10):
            slot = u % 2
            f = step * 10 + u
            block = w1[:, pl.ds(pl.multiple_of(f * 256, 256), 256)]
            for a in range(3):
                y = jnp.dot(x[a * count : (a + 1) * count, :], block, preferred_element_type=F32)
                ycat[slot, 0:count, 256 * a : 256 * a + 256] = jnp.maximum(y, 0.0).astype(BF16)
            r = jnp.dot(ycat[slot, 0:count, :], w2[...], preferred_element_type=F32)
            out = jnp.maximum(r[:, :CH] + lower[slot, 0:count, :] + bias, 0.0).astype(BF16)
            lower[1 - slot, 0:count, :] = r[:, CH:]
            second_out[0:count, pl.ds(pl.multiple_of(f * CH, CH), CH)] = out
        return carry

    lax.fori_loop(0, BINS // 10, body, 0)


def embed_rows(begin, count, second_out, embed_w, embedded):
    embedded[begin : begin + count, :] = jnp.dot(
        second_out[0:count, :], embed_w[...], preferred_element_type=F32
    ).astype(BF16)


def norm_rows(begin, count, embedded, gain, normed):
    def step(r, carry):
        rows = pl.ds(pl.multiple_of(begin + r * 64, 64), 64)
        values = embedded[rows, :].astype(F32)
        center = values - jnp.mean(values, axis=1, keepdims=True)
        spread = jnp.mean(center * center, axis=1, keepdims=True)
        normed[rows, :] = (center * lax.rsqrt(spread + 1e-05) * gain[...]).astype(BF16)
        return carry

    lax.fori_loop(0, count // 64, step, 0)


def build_hide(device, devices, base, starts, hide):
    spots = device * SHARD - CTX + lax.broadcasted_iota(jnp.int32, (1, KEY_ROWS), 1)
    key_code = codes(*locate(spots, base, starts))
    key_code = jnp.where((spots >= 0) & (spots < devices * SHARD), key_code, -1000)
    for block in range(SHARD // QB):
        q_spots = device * SHARD + block * QB + lax.broadcasted_iota(jnp.int32, (QB, 1), 0)
        q_code = codes(*locate(q_spots, base, starts))
        gap = q_code - key_code[:, block * QB : block * QB + QK]
        hide[block] = jnp.where((gap >= 0) & (gap <= LEFT_SPANS), 0.0, -1e30)


def attend_block(block, queries, keys, vals, hide, mixed):
    rows = pl.ds(pl.multiple_of(block * QB, QB), QB)
    k_rows = pl.ds(pl.multiple_of(block * QB, QB), QK)
    left = lax.broadcasted_iota(jnp.int32, (QB, CH), 1) < 64
    ones = jnp.ones((QK, CH), BF16)
    for pair in range(D // CH):
        cols = slice(pair * CH, pair * CH + CH)
        q = queries[rows, cols]
        v = jnp.concatenate([vals[k_rows, cols], ones], axis=1)
        outs = []
        for half in (left, jnp.logical_not(left)):
            s = lax.dot_general(
                jnp.where(half, q, BF16(0)),
                keys[k_rows, cols],
                (((1,), (1,)), ((), ())),
                preferred_element_type=F32,
            )
            s = s + hide[block]
            p = jnp.exp(s - jnp.max(s, axis=1, keepdims=True)).astype(BF16)
            o = jnp.dot(p, v, preferred_element_type=F32)
            outs.append(o[:, :CH] / o[:, CH:])
        mixed[rows, cols] = jnp.where(left, outs[0], outs[1]).astype(BF16)


def context_rows(src, target, count, head_w, keys, vals):
    rows = slice(target, target + count)
    keys[rows, :] = jnp.dot(src, head_w[:, D : 2 * D], preferred_element_type=F32).astype(BF16)
    vals[rows, :] = jnp.dot(src, head_w[:, 2 * D :], preferred_element_type=F32).astype(BF16)


def layer_kernel(
    raw_hbm,
    lens_ref,
    lens_smem,
    first_kernel,
    first_bias,
    second_kernel,
    second_bias,
    gain,
    embed_hbm,
    head_hbm,
    out_hbm,
    encoded,
    raw,
    low,
    high,
    kext,
    w1,
    w2,
    rows32,
    x_late,
    x_early,
    ycat,
    lower,
    second_out,
    embed_w,
    head_w,
    out_w,
    embedded,
    normed,
    before,
    after,
    queries,
    keys,
    vals,
    mixed,
    hide,
    load_sems,
    send_sems,
    recv_sems,
):
    inner = lax.axis_size("inner")
    devices = lax.axis_size("seq") * inner
    device = lax.axis_index("seq") * inner + lax.axis_index("inner")
    right_id = lax.rem(device + 1, devices)
    left_id = lax.rem(device + devices - 1, devices)
    right = (right_id // inner, lax.rem(right_id, inner))
    left = (left_id // inner, lax.rem(left_id, inner))
    barrier = pltpu.get_barrier_semaphore()
    for neighbour in (left, right):
        pl.semaphore_signal(barrier, inc=1, device_id=neighbour, device_id_type=MESH)

    def load(source, target, index):
        copy = pltpu.make_async_copy(source, target, load_sems.at[index])
        copy.start()
        return copy

    def send(source, target, index, neighbour):
        copy = pltpu.make_async_remote_copy(
            src_ref=source,
            dst_ref=target,
            send_sem=send_sems.at[index],
            recv_sem=recv_sems.at[index],
            device_id=neighbour,
            device_id_type=MESH,
        )
        copy.start()
        return copy

    load_raw = load(raw_hbm, raw, 0)
    pl.semaphore_wait(barrier, 2)
    cap = raw_hbm.shape[1]
    send_low = send(raw_hbm.at[:, cap - SIDE : cap], low, 0, right)
    send_high = send(raw_hbm.at[:, 0:SIDE], high, 1, left)
    load_embed = load(embed_hbm, embed_w, 1)
    load_head = load(head_hbm, head_w, 2)
    load_out = load(out_hbm, out_w, 3)
    base, starts = bounds(device, devices, lens_ref, lens_smem)
    build_taps(first_kernel, first_bias, kext)
    build_first(kext, w1)
    build_second(second_kernel, w2)
    build_hide(device, devices, base, starts, hide)
    spots = device * SHARD + lax.broadcasted_iota(jnp.int32, (SHARD, 1), 0)
    unused_seg, pos = locate(spots, base, starts)
    joined = pos > 0
    load_raw.wait()
    send_low.wait_recv()
    send_high.wait_recv()
    select_rows(device, base, starts, raw, low, high, rows32)
    build_inputs(CUT, SHARD - CUT, joined, rows32, x_late)
    build_inputs(0, CUT, joined, rows32, x_early)

    convolve(SHARD - CUT, x_late, w1, w2, second_bias, ycat, lower, second_out)
    load_embed.wait()
    embed_rows(CUT, SHARD - CUT, second_out, embed_w, embedded)
    norm_rows(CUT, SHARD - CUT, embedded, gain, normed)
    send_tail = send(normed.at[SHARD - SPAN : SHARD, :], before.at[CTX - SPAN : CTX, :], 2, right)
    send_body = send(normed.at[SHARD - CTX : SHARD - SPAN, :], before.at[0 : CTX - SPAN, :], 3, right)

    convolve(CUT, x_early, w1, w2, second_bias, ycat, lower, second_out)
    embed_rows(0, CUT, second_out, embed_w, embedded)
    norm_rows(0, CUT, embedded, gain, normed)
    send_head = send(normed.at[0:SPAN, :], after, 4, left)

    load_head.wait()
    queries[...] = (
        jnp.dot(normed[...], head_w[:, 0:D], preferred_element_type=F32).astype(BF16) * BF16(0.125)
    )
    context_rows(normed[...], CTX, SHARD, head_w, keys, vals)
    send_tail.wait_recv()
    send_head.wait_recv()
    context_rows(after[...], CTX + SHARD, SPAN, head_w, keys, vals)
    context_rows(before[CTX - SPAN : CTX, :], CTX - SPAN, SPAN, head_w, keys, vals)

    def block_step(step, carry):
        @pl.when(step == 2)
        def rest():
            send_body.wait_recv()
            context_rows(before[0 : CTX - SPAN, :], 0, CTX - SPAN, head_w, keys, vals)

        attend_block(3 - step, queries, keys, vals, hide, mixed)
        return carry

    lax.fori_loop(0, SHARD // QB, block_step, 0)
    load_out.wait()
    encoded[...] = (
        embedded[...].astype(F32) + jnp.dot(mixed[...], out_w[...], preferred_element_type=F32)
    ).astype(BF16)
    for copy in (send_low, send_high, send_tail, send_body, send_head):
        copy.wait_send()


def on_device(
    log_mel,
    lengths,
    first_kernel,
    first_bias,
    second_kernel,
    second_bias,
    embed_weight,
    norm_gain,
    head_weight,
    output_weight,
):
    vmem = pl.BlockSpec(memory_space=pltpu.VMEM)
    smem = pl.BlockSpec(memory_space=pltpu.SMEM)
    hbm = pl.BlockSpec(memory_space=pl.ANY)
    late = SHARD - CUT
    return pl.pallas_call(
        layer_kernel,
        out_shape=jax.ShapeDtypeStruct((SHARD, D), BF16),
        in_specs=[hbm, vmem, smem, vmem, vmem, vmem, vmem, vmem, hbm, hbm, hbm],
        out_specs=vmem,
        scratch_shapes=[
            pltpu.VMEM((4 * MEL, log_mel.shape[0]), BF16),
            pltpu.VMEM((4 * MEL, SIDE), BF16),
            pltpu.VMEM((4 * MEL, SIDE), BF16),
            pltpu.VMEM((32, 256), F32),
            pltpu.VMEM((256, BINS * 256), BF16),
            pltpu.VMEM((768, 256), BF16),
            pltpu.VMEM((WIDE, 4 * MEL), F32),
            pltpu.VMEM((3 * late, 256), BF16),
            pltpu.VMEM((3 * CUT, 256), BF16),
            pltpu.VMEM((2, late, 768), BF16),
            pltpu.VMEM((2, late, CH), F32),
            pltpu.VMEM((late, BINS * CH), BF16),
            pltpu.VMEM((BINS * CH, D), BF16),
            pltpu.VMEM((D, 3 * D), BF16),
            pltpu.VMEM((D, D), BF16),
            pltpu.VMEM((SHARD, D), BF16),
            pltpu.VMEM((SHARD, D), BF16),
            pltpu.VMEM((CTX, D), BF16),
            pltpu.VMEM((SPAN, D), BF16),
            pltpu.VMEM((SHARD, D), BF16),
            pltpu.VMEM((KEY_ROWS, D), BF16),
            pltpu.VMEM((KEY_ROWS, D), BF16),
            pltpu.VMEM((SHARD, D), BF16),
            pltpu.VMEM((SHARD // QB, QB, QK), F32),
            pltpu.SemaphoreType.DMA((4,)),
            pltpu.SemaphoreType.DMA((5,)),
            pltpu.SemaphoreType.DMA((5,)),
        ],
        compiler_params=pltpu.CompilerParams(
            vmem_limit_bytes=56 * 2**20, collective_id=0, has_side_effects=True
        ),
        name="layer",
    )(
        log_mel.T,
        lengths.T,
        lengths.T,
        first_kernel,
        first_bias.reshape(1, -1),
        second_kernel,
        second_bias.reshape(1, -1),
        norm_gain.reshape(1, -1),
        embed_weight,
        head_weight,
        output_weight,
    )


def solution(mesh):
    return jax.shard_map(
        on_device,
        mesh=mesh,
        in_specs=(P(AXES, None), P(), P(), P(), P(), P(), P(), P(), P(), P()),
        out_specs=P(AXES, None),
        check_vma=False,
    )
```

```python
import jax
import jax.numpy as jnp
from jax import lax
from jax.experimental import pallas as pl
from jax.experimental.pallas import tpu as pltpu
from jax.sharding import PartitionSpec as P

SPAN = 64
LEFT_SPANS = 4
CTX = 320
SHARD = 512
MARGIN = 192
MEL = 80
CH = 128
D = 1024
BINS = 20
CUT = 192
MIDDLE = 128
SIDE = 256
QB = 128
QK = 512
KEY_ROWS = CTX + SHARD + SPAN
AXES = ("seq", "inner")
F32 = jnp.float32
BF16 = jnp.bfloat16
MESH = pl.DeviceIdType.MESH


def bounds(device, devices, lens_ref, lens_smem):
    owners = lax.broadcasted_iota(jnp.int32, lens_ref.shape, 1)
    before = jnp.where(owners < device - 1, lens_ref[...].astype(F32), 0.0)
    base = jnp.sum(jnp.sum(before, axis=0, keepdims=True), axis=1, keepdims=True).astype(jnp.int32)
    starts = []
    total = jnp.int32(0)
    for step in (-1, 0, 1):
        owner = device + step
        real = (owner >= 0) & (owner < devices)
        safe = lax.rem(owner + devices, devices)
        for column in range(lens_smem.shape[0]):
            starts.append(total)
            total = total + jnp.where(real, lens_smem[column, safe], 0)
    return base, starts


def locate(spots, base, starts):
    rel = spots - base
    seg = jnp.zeros_like(rel)
    begin = jnp.zeros_like(rel)
    for start in starts[1:]:
        reached = rel >= start
        seg = seg + reached.astype(jnp.int32)
        begin = jnp.where(reached, start, begin)
    return seg, rel - begin


def codes(seg, pos):
    return seg * 64 + lax.shift_right_arithmetic(pos, 6)


def build_taps(first_kernel, first_bias, kext):
    kext[...] = jnp.zeros_like(kext)
    taps = first_kernel[...].astype(F32)
    for a in range(3):
        for b in range(3):
            row = taps[3 * a + b : 3 * a + b + 1, :]
            kext[5 * a + b : 5 * a + b + 1, 0:CH] = row
            kext[5 * a + b + 2 : 5 * a + b + 3, CH : 2 * CH] = row
    rest = first_bias[...]
    for part in range(3):
        piece = rest.astype(BF16).astype(F32)
        rest = rest - piece
        kext[15 + part : 16 + part, 0:CH] = piece
        kext[15 + part : 16 + part, CH : 2 * CH] = piece


def build_first(kext, w1):
    row = lax.broadcasted_iota(jnp.int32, (256, 32), 0)
    col = lax.broadcasted_iota(jnp.int32, (256, 32), 1)
    tap = (row >= MEL).astype(jnp.int32) + (row >= 2 * MEL).astype(jnp.int32)
    mel = row - MEL * tap
    wide = kext[...].astype(BF16)

    def body(f, carry):
        off = mel - 4 * f + 1
        inside = (off >= 0) & (off <= 4) & (row < 3 * MEL)
        want = jnp.where(inside, 5 * tap + off, jnp.where(row >= 3 * MEL, row - 3 * MEL + 15, -1))
        select = jnp.where(col == want, 1.0, 0.0).astype(BF16)
        block = jnp.dot(select, wide, preferred_element_type=F32)
        w1[:, pl.ds(pl.multiple_of(f * 256, 256), 256)] = block.astype(BF16)
        return carry

    lax.fori_loop(0, BINS, body, 0, unroll=4)


def build_second(second_kernel, w2):
    for a in range(3):
        base = 3 * a * CH
        w2[256 * a : 256 * a + 256, 0:CH] = second_kernel[base + CH : base + 3 * CH, :]
        w2[256 * a : 256 * a + CH, CH : 2 * CH] = jnp.zeros((CH, CH), BF16)
        w2[256 * a + CH : 256 * a + 256, CH : 2 * CH] = second_kernel[base : base + CH, :]


def pick(device, base, starts, first, far, owner_index, near):
    spots = device * SHARD + first + lax.broadcasted_iota(jnp.int32, (1, SIDE), 1)
    seg, unused_pos = locate(spots, base, starts)
    owner = lax.shift_right_arithmetic(seg, 2)
    return jnp.where(owner == owner_index, far[...].astype(F32), near.astype(F32))


def build_inputs(offset, begin, count, joined, rows32, x):
    here = joined[begin : begin + count]
    now = rows32[offset : offset + count, :]
    before = jnp.where(here, rows32[offset - 1 : offset + count - 1, :], 0.0)
    ones = jnp.ones((count, 16), F32)
    kept = jnp.where(here, ones, 0.0)
    x[0:count, :] = jnp.concatenate([before[:, MEL:], kept], axis=1).astype(BF16)
    x[count : 2 * count, :] = jnp.concatenate(
        [before[:, 3 * MEL :], now[:, : 2 * MEL], ones], axis=1
    ).astype(BF16)
    x[2 * count : 3 * count, :] = jnp.concatenate([now[:, MEL:], ones], axis=1).astype(BF16)


def convolve(begin, count, x, w1, w2, second_bias, ycat, second_out):
    bias = second_bias[...]
    lower = None
    for f in range(BINS):
        slot = f % 2
        y = jnp.dot(x[0 : 3 * count, :], w1[:, 256 * f : 256 * f + 256], preferred_element_type=F32)
        for a in range(3):
            ycat[slot, 0:count, 256 * a : 256 * a + 256] = jnp.maximum(
                y[a * count : (a + 1) * count], 0.0
            ).astype(BF16)
        r = jnp.dot(ycat[slot, 0:count, :], w2[...], preferred_element_type=F32)
        total = r[:, :CH] + bias if lower is None else r[:, :CH] + lower + bias
        lower = r[:, CH:]
        second_out[begin : begin + count, CH * f : CH * f + CH] = jnp.maximum(total, 0.0).astype(BF16)


def embed_rows(begin, count, second_out, embed_w, embedded):
    embedded[begin : begin + count, :] = jnp.dot(
        second_out[0:count, :], embed_w[...], preferred_element_type=F32
    ).astype(BF16)


def norm_rows(begin, count, embedded, gain, normed):
    def step(r, carry):
        rows = pl.ds(pl.multiple_of(begin + r * 64, 64), 64)
        values = embedded[rows, :].astype(F32)
        center = values - jnp.mean(values, axis=1, keepdims=True)
        spread = jnp.mean(center * center, axis=1, keepdims=True)
        normed[rows, :] = (center * lax.rsqrt(spread + 1e-05) * gain[...]).astype(BF16)
        return carry

    lax.fori_loop(0, count // 64, step, 0)


def build_hide(device, devices, base, starts, hide):
    spots = device * SHARD - CTX + lax.broadcasted_iota(jnp.int32, (1, KEY_ROWS), 1)
    key_code = codes(*locate(spots, base, starts))
    key_code = jnp.where((spots >= 0) & (spots < devices * SHARD), key_code, -1000)
    for block in range(SHARD // QB):
        q_spots = device * SHARD + block * QB + lax.broadcasted_iota(jnp.int32, (QB, 1), 0)
        q_code = codes(*locate(q_spots, base, starts))
        gap = q_code - key_code[:, block * QB : block * QB + QK]
        hide[block] = jnp.where((gap >= 0) & (gap <= LEFT_SPANS), 0.0, -1e30)


def attend_block(block, queries, keys, vals, hide, mixed):
    rows = pl.ds(pl.multiple_of(block * QB, QB), QB)
    k_rows = pl.ds(pl.multiple_of(block * QB, QB), QK)
    left = lax.broadcasted_iota(jnp.int32, (QB, CH), 1) < 64
    ones = jnp.ones((QK, CH), BF16)
    for pair in range(D // CH):
        cols = slice(pair * CH, pair * CH + CH)
        q = queries[rows, cols]
        v = jnp.concatenate([vals[k_rows, cols], ones], axis=1)
        outs = []
        for half in (left, jnp.logical_not(left)):
            s = lax.dot_general(
                jnp.where(half, q, BF16(0)),
                keys[k_rows, cols],
                (((1,), (1,)), ((), ())),
                preferred_element_type=F32,
            )
            s = s + hide[block]
            p = jnp.exp(s - jnp.max(s, axis=1, keepdims=True)).astype(BF16)
            o = jnp.dot(p, v, preferred_element_type=F32)
            outs.append(o[:, :CH] / o[:, CH:])
        mixed[rows, cols] = jnp.where(left, outs[0], outs[1]).astype(BF16)


def context_rows(src, target, count, head_w, keys, vals):
    rows = slice(target, target + count)
    keys[rows, :] = jnp.dot(src, head_w[:, D : 2 * D], preferred_element_type=F32).astype(BF16)
    vals[rows, :] = jnp.dot(src, head_w[:, 2 * D :], preferred_element_type=F32).astype(BF16)


def layer_kernel(
    raw_hbm,
    lens_hbm,
    taps_hbm,
    first_bias_hbm,
    second_hbm,
    second_bias_hbm,
    gain_hbm,
    embed_hbm,
    head_hbm,
    out_hbm,
    encoded,
    raw,
    low,
    high,
    lens_ref,
    lens_smem,
    first_kernel,
    first_bias,
    second_kernel,
    second_bias,
    gain,
    kext,
    w1,
    w2,
    rows32,
    x,
    ycat,
    second_out,
    embed_w,
    head_w,
    out_w,
    embedded,
    normed,
    before,
    after,
    queries,
    keys,
    vals,
    mixed,
    hide,
    load_sems,
    send_sems,
    recv_sems,
):
    inner = lax.axis_size("inner")
    devices = lax.axis_size("seq") * inner
    device = lax.axis_index("seq") * inner + lax.axis_index("inner")
    has_left = device > 0
    has_right = device < devices - 1
    right_id = lax.rem(device + 1, devices)
    left_id = lax.rem(device + devices - 1, devices)
    right = (right_id // inner, lax.rem(right_id, inner))
    left = (left_id // inner, lax.rem(left_id, inner))
    barrier = pltpu.get_barrier_semaphore()

    @pl.when(has_left)
    def greet_left():
        pl.semaphore_signal(barrier, inc=1, device_id=left, device_id_type=MESH)

    @pl.when(has_right)
    def greet_right():
        pl.semaphore_signal(barrier, inc=1, device_id=right, device_id_type=MESH)

    def load(source, target, index):
        copy = pltpu.make_async_copy(source, target, load_sems.at[index])
        copy.start()
        return copy

    def remote(source, target, index, neighbour):
        return pltpu.make_async_remote_copy(
            src_ref=source,
            dst_ref=target,
            send_sem=send_sems.at[index],
            recv_sem=recv_sems.at[index],
            device_id=neighbour,
            device_id_type=MESH,
        )

    small = [
        load(source, target, index)
        for index, (source, target) in enumerate(
            (
                (lens_hbm, lens_ref),
                (lens_hbm, lens_smem),
                (taps_hbm, first_kernel),
                (first_bias_hbm, first_bias),
                (second_hbm, second_kernel),
                (second_bias_hbm, second_bias),
                (gain_hbm, gain),
            )
        )
    ]
    load_raw = load(raw_hbm, raw, 7)
    cap = raw_hbm.shape[1]
    send_low = remote(raw_hbm.at[:, cap - SIDE : cap], low, 0, right)
    send_high = remote(raw_hbm.at[:, 0:SIDE], high, 1, left)
    send_tail = remote(
        normed.at[SHARD - SPAN : SHARD, :], before.at[CTX - SPAN : CTX, :], 2, right
    )
    send_body = remote(
        normed.at[SHARD - CTX : SHARD - SPAN, :], before.at[0 : CTX - SPAN, :], 3, right
    )
    send_head = remote(normed.at[0:SPAN, :], after, 4, left)

    @pl.when(jnp.logical_not(has_left))
    def clear_left():
        low[...] = jnp.zeros_like(low)
        before[...] = jnp.zeros_like(before)

    @pl.when(jnp.logical_not(has_right))
    def clear_right():
        high[...] = jnp.zeros_like(high)
        after[...] = jnp.zeros_like(after)

    @pl.when(has_left & has_right)
    def meet_both():
        pl.semaphore_wait(barrier, 2)

    @pl.when(jnp.logical_not(has_left & has_right))
    def meet_one():
        pl.semaphore_wait(barrier, 1)

    @pl.when(has_right)
    def start_low():
        send_low.start()

    @pl.when(has_left)
    def start_high():
        send_high.start()

    load_embed = load(embed_hbm, embed_w, 8)
    load_head = load(head_hbm, head_w, 9)
    load_out = load(out_hbm, out_w, 10)
    for copy in small:
        copy.wait()
    base, starts = bounds(device, devices, lens_ref, lens_smem)
    build_taps(first_kernel, first_bias, kext)
    build_first(kext, w1)
    build_second(second_kernel, w2)
    build_hide(device, devices, base, starts, hide)
    spots = device * SHARD + lax.broadcasted_iota(jnp.int32, (SHARD, 1), 0)
    unused_seg, pos = locate(spots, base, starts)
    joined = pos > 0
    load_raw.wait()
    rows32[0:256, :] = raw[:, 256:512].astype(F32).T
    build_inputs(128, CUT, MIDDLE, joined, rows32, x)
    convolve(0, MIDDLE, x, w1, w2, second_bias, ycat, second_out)

    @pl.when(has_right)
    def land_high():
        send_high.wait_recv()

    far = pick(device, base, starts, CTX, high, 2, raw[:, 512:768])
    rows32[...] = jnp.concatenate([raw[:, 384:512].astype(F32), far], axis=1).T
    build_inputs(128, CTX, CUT, joined, rows32, x)
    convolve(MIDDLE, CUT, x, w1, w2, second_bias, ycat, second_out)
    load_embed.wait()
    embed_rows(CUT, CTX, second_out, embed_w, embedded)
    norm_rows(CUT, CTX, embedded, gain, normed)

    @pl.when(has_right)
    def start_context():
        send_tail.start()
        send_body.start()

    @pl.when(has_left)
    def land_low():
        send_low.wait_recv()

    rows32[0:256, :] = pick(device, base, starts, -64, low, 0, raw[:, 128:384]).T
    build_inputs(64, 0, CUT, joined, rows32, x)
    convolve(0, CUT, x, w1, w2, second_bias, ycat, second_out)
    embed_rows(0, CUT, second_out, embed_w, embedded)
    norm_rows(0, CUT, embedded, gain, normed)

    @pl.when(has_left)
    def start_after():
        send_head.start()

    load_head.wait()
    queries[...] = (
        jnp.dot(normed[...], head_w[:, 0:D], preferred_element_type=F32).astype(BF16) * BF16(0.125)
    )
    context_rows(normed[...], CTX, SHARD, head_w, keys, vals)

    @pl.when(has_left)
    def land_tail():
        send_tail.wait_recv()

    @pl.when(has_right)
    def land_after():
        send_head.wait_recv()

    context_rows(after[...], CTX + SHARD, SPAN, head_w, keys, vals)
    context_rows(before[CTX - SPAN : CTX, :], CTX - SPAN, SPAN, head_w, keys, vals)

    def block_step(step, carry):
        @pl.when((step == 2) & has_left)
        def land_body():
            send_body.wait_recv()

        @pl.when(step == 2)
        def rest():
            context_rows(before[0 : CTX - SPAN, :], 0, CTX - SPAN, head_w, keys, vals)

        attend_block(3 - step, queries, keys, vals, hide, mixed)
        return carry

    lax.fori_loop(0, SHARD // QB, block_step, 0)
    load_out.wait()
    encoded[...] = (
        embedded[...].astype(F32) + jnp.dot(mixed[...], out_w[...], preferred_element_type=F32)
    ).astype(BF16)

    @pl.when(has_right)
    def sent_right():
        send_low.wait_send()
        send_tail.wait_send()
        send_body.wait_send()

    @pl.when(has_left)
    def sent_left():
        send_high.wait_send()
        send_head.wait_send()


def on_device(
    log_mel,
    lengths,
    first_kernel,
    first_bias,
    second_kernel,
    second_bias,
    embed_weight,
    norm_gain,
    head_weight,
    output_weight,
):
    hbm = pl.BlockSpec(memory_space=pl.ANY)
    return pl.pallas_call(
        layer_kernel,
        out_shape=jax.ShapeDtypeStruct((SHARD, D), BF16),
        in_specs=[hbm] * 10,
        out_specs=pl.BlockSpec(memory_space=pltpu.VMEM),
        scratch_shapes=[
            pltpu.VMEM((4 * MEL, log_mel.shape[0]), BF16),
            pltpu.VMEM((4 * MEL, SIDE), BF16),
            pltpu.VMEM((4 * MEL, SIDE), BF16),
            pltpu.VMEM(lengths.shape[::-1], jnp.int32),
            pltpu.SMEM(lengths.shape[::-1], jnp.int32),
            pltpu.VMEM((9, CH), BF16),
            pltpu.VMEM((1, CH), F32),
            pltpu.VMEM((9 * CH, CH), BF16),
            pltpu.VMEM((1, CH), F32),
            pltpu.VMEM((1, D), F32),
            pltpu.VMEM((32, 256), F32),
            pltpu.VMEM((256, BINS * 256), BF16),
            pltpu.VMEM((768, 256), BF16),
            pltpu.VMEM((2 * CUT, 4 * MEL), F32),
            pltpu.VMEM((3 * CUT, 256), BF16),
            pltpu.VMEM((2, CUT, 768), BF16),
            pltpu.VMEM((CTX, BINS * CH), BF16),
            pltpu.VMEM((BINS * CH, D), BF16),
            pltpu.VMEM((D, 3 * D), BF16),
            pltpu.VMEM((D, D), BF16),
            pltpu.VMEM((SHARD, D), BF16),
            pltpu.VMEM((SHARD, D), BF16),
            pltpu.VMEM((CTX, D), BF16),
            pltpu.VMEM((SPAN, D), BF16),
            pltpu.VMEM((SHARD, D), BF16),
            pltpu.VMEM((KEY_ROWS, D), BF16),
            pltpu.VMEM((KEY_ROWS, D), BF16),
            pltpu.VMEM((SHARD, D), BF16),
            pltpu.VMEM((SHARD // QB, QB, QK), F32),
            pltpu.SemaphoreType.DMA((11,)),
            pltpu.SemaphoreType.DMA((5,)),
            pltpu.SemaphoreType.DMA((5,)),
        ],
        compiler_params=pltpu.CompilerParams(
            vmem_limit_bytes=56 * 2**20, collective_id=0, has_side_effects=True
        ),
        name="layer",
    )(
        log_mel.T,
        lengths.T,
        first_kernel,
        first_bias.reshape(1, -1),
        second_kernel,
        second_bias.reshape(1, -1),
        norm_gain.reshape(1, -1),
        embed_weight,
        head_weight,
        output_weight,
    )


def solution(mesh):
    return jax.shard_map(
        on_device,
        mesh=mesh,
        in_specs=(P(AXES, None), P(), P(), P(), P(), P(), P(), P(), P(), P()),
        out_specs=P(AXES, None),
        check_vma=False,
    )
```

```python
import jax
import jax.numpy as jnp
from jax import lax
from jax.experimental import pallas as pl
from jax.experimental.pallas import tpu as pltpu
from jax.sharding import PartitionSpec as P

SPAN = 64
LEFT_SPANS = 4
CTX = 320
SHARD = 512
MARGIN = 192
MEL = 80
CH = 128
D = 1024
BINS = 20
CUT = 192
MIDDLE = 128
SIDE = 256
QB = 128
QK = 512
KEY_ROWS = CTX + SHARD + SPAN
AXES = ("seq", "inner")
F32 = jnp.float32
BF16 = jnp.bfloat16
MESH = pl.DeviceIdType.MESH


def bounds(device, devices, lens_ref, lens_smem):
    owners = lax.broadcasted_iota(jnp.int32, lens_ref.shape, 1)
    before = jnp.where(owners < device - 1, lens_ref[...].astype(F32), 0.0)
    base = jnp.sum(jnp.sum(before, axis=0, keepdims=True), axis=1, keepdims=True).astype(jnp.int32)
    starts = []
    total = jnp.int32(0)
    for step in (-1, 0, 1):
        owner = device + step
        real = (owner >= 0) & (owner < devices)
        safe = lax.rem(owner + devices, devices)
        for column in range(lens_smem.shape[0]):
            starts.append(total)
            total = total + jnp.where(real, lens_smem[column, safe], 0)
    return base, starts


def locate(spots, base, starts):
    rel = spots - base
    seg = jnp.zeros_like(rel)
    begin = jnp.zeros_like(rel)
    for start in starts[1:]:
        reached = rel >= start
        seg = seg + reached.astype(jnp.int32)
        begin = jnp.where(reached, start, begin)
    return seg, rel - begin


def codes(seg, pos):
    return seg * 64 + lax.shift_right_arithmetic(pos, 6)


def build_taps(first_kernel, first_bias, kext):
    kext[...] = jnp.zeros_like(kext)
    taps = first_kernel[...].astype(F32)
    for a in range(3):
        for b in range(3):
            row = taps[3 * a + b : 3 * a + b + 1, :]
            kext[5 * a + b : 5 * a + b + 1, 0:CH] = row
            kext[5 * a + b + 2 : 5 * a + b + 3, CH : 2 * CH] = row
    rest = first_bias[...]
    for part in range(3):
        piece = rest.astype(BF16).astype(F32)
        rest = rest - piece
        kext[15 + part : 16 + part, 0:CH] = piece
        kext[15 + part : 16 + part, CH : 2 * CH] = piece


def build_first(kext, w1):
    row = lax.broadcasted_iota(jnp.int32, (256, 32), 0)
    col = lax.broadcasted_iota(jnp.int32, (256, 32), 1)
    tap = (row >= MEL).astype(jnp.int32) + (row >= 2 * MEL).astype(jnp.int32)
    off = col - 5 * tap
    inside = (off >= 0) & (off <= 4) & (row < 3 * MEL)
    when = jnp.where(inside, row - MEL * tap + 1 - off, -1)
    always = jnp.where((row >= 3 * MEL) & (row - 3 * MEL + 15 == col), 1.0, 0.0)
    wide = kext[...].astype(BF16)
    for f in range(BINS):
        select = jnp.where(when == 4 * f, 1.0, always).astype(BF16)
        block = jnp.dot(select, wide, preferred_element_type=F32)
        w1[:, 256 * f : 256 * f + 256] = block.astype(BF16)


def build_second(second_kernel, w2):
    for a in range(3):
        base = 3 * a * CH
        w2[256 * a : 256 * a + 256, 0:CH] = second_kernel[base + CH : base + 3 * CH, :]
        w2[256 * a : 256 * a + CH, CH : 2 * CH] = jnp.zeros((CH, CH), BF16)
        w2[256 * a + CH : 256 * a + 256, CH : 2 * CH] = second_kernel[base : base + CH, :]


def pick(device, base, starts, first, far, owner_index, near):
    spots = device * SHARD + first + lax.broadcasted_iota(jnp.int32, (1, SIDE), 1)
    seg, unused_pos = locate(spots, base, starts)
    owner = lax.shift_right_arithmetic(seg, 2)
    return jnp.where(owner == owner_index, far[...].astype(F32), near.astype(F32))


def build_inputs(offset, begin, count, joined, rows32, x):
    here = joined[begin : begin + count]
    now = rows32[offset : offset + count, :]
    before = jnp.where(here, rows32[offset - 1 : offset + count - 1, :], 0.0)
    ones = jnp.ones((count, 16), F32)
    kept = jnp.where(here, ones, 0.0)
    x[0:count, :] = jnp.concatenate([before[:, MEL:], kept], axis=1).astype(BF16)
    x[count : 2 * count, :] = jnp.concatenate(
        [before[:, 3 * MEL :], now[:, : 2 * MEL], ones], axis=1
    ).astype(BF16)
    x[2 * count : 3 * count, :] = jnp.concatenate([now[:, MEL:], ones], axis=1).astype(BF16)


def convolve(begin, count, x, w1, w2, second_bias, ycat, second_out):
    bias = second_bias[...]
    lower = None
    for f in range(BINS):
        slot = f % 2
        y = jnp.dot(x[0 : 3 * count, :], w1[:, 256 * f : 256 * f + 256], preferred_element_type=F32)
        for a in range(3):
            ycat[slot, 0:count, 256 * a : 256 * a + 256] = jnp.maximum(
                y[a * count : (a + 1) * count], 0.0
            ).astype(BF16)
        r = jnp.dot(ycat[slot, 0:count, :], w2[...], preferred_element_type=F32)
        total = r[:, :CH] + bias if lower is None else r[:, :CH] + lower + bias
        lower = r[:, CH:]
        second_out[begin : begin + count, CH * f : CH * f + CH] = jnp.maximum(total, 0.0).astype(BF16)


def embed_rows(begin, count, second_out, embed_w, embedded):
    embedded[begin : begin + count, :] = jnp.dot(
        second_out[0:count, :], embed_w[...], preferred_element_type=F32
    ).astype(BF16)


def norm_rows(begin, count, embedded, gain, normed):
    for r in range(begin, begin + count, 64):
        values = embedded[r : r + 64, :].astype(F32)
        center = values - jnp.mean(values, axis=1, keepdims=True)
        spread = jnp.mean(center * center, axis=1, keepdims=True)
        normed[CTX + r : CTX + r + 64, :] = (
            center * lax.rsqrt(spread + 1e-05) * gain[...]
        ).astype(BF16)


def build_hide(device, devices, base, starts, hide):
    spots = device * SHARD - CTX + lax.broadcasted_iota(jnp.int32, (1, KEY_ROWS), 1)
    key_code = codes(*locate(spots, base, starts))
    key_code = jnp.where((spots >= 0) & (spots < devices * SHARD), key_code, -1000)
    for block in range(SHARD // QB):
        q_spots = device * SHARD + block * QB + lax.broadcasted_iota(jnp.int32, (QB, 1), 0)
        q_code = codes(*locate(q_spots, base, starts))
        gap = q_code - key_code[:, block * QB : block * QB + QK]
        hide[block] = jnp.where((gap >= 0) & (gap <= LEFT_SPANS), 0.0, -1e30)


def project(block, piece, mixed, embedded, out_w, encoded):
    rows = slice(block * QB, block * QB + QB)
    cols = slice(piece * 256, piece * 256 + 256)
    total = jnp.dot(mixed[rows, :], out_w[:, cols], preferred_element_type=F32)
    encoded[rows, cols] = (embedded[rows, cols].astype(F32) + total).astype(BF16)


def attend_block(block, done, queries, keys, vals, hide, mixed, embedded, out_w, encoded):
    rows = slice(block * QB, block * QB + QB)
    k_rows = slice(block * QB, block * QB + QK)
    left = lax.broadcasted_iota(jnp.int32, (QB, CH), 1) < 64
    ones = jnp.ones((QK, CH), BF16)
    for pair in range(D // CH):
        cols = slice(pair * CH, pair * CH + CH)
        q = queries[rows, cols]
        v = jnp.concatenate([vals[k_rows, cols], ones], axis=1)
        outs = []
        for half in (left, jnp.logical_not(left)):
            s = lax.dot_general(
                jnp.where(half, q, BF16(0)),
                keys[k_rows, cols],
                (((1,), (1,)), ((), ())),
                preferred_element_type=F32,
            )
            s = s + hide[block]
            p = jnp.exp(s - jnp.max(s, axis=1, keepdims=True)).astype(BF16)
            o = jnp.dot(p, v, preferred_element_type=F32)
            outs.append(o[:, :CH] / o[:, CH:])
        mixed[rows, cols] = jnp.where(left, outs[0], outs[1]).astype(BF16)
        if done is not None and pair % 2 == 1:
            project(done, pair // 2, mixed, embedded, out_w, encoded)


def head_rows(src, column, head_w):
    return jnp.dot(src, head_w[:, column : column + D], preferred_element_type=F32).astype(BF16)


def layer_kernel(
    raw_hbm,
    lens_hbm,
    taps_hbm,
    first_bias_hbm,
    second_hbm,
    second_bias_hbm,
    gain_hbm,
    embed_hbm,
    head_hbm,
    out_hbm,
    encoded,
    raw,
    low,
    high,
    lens_ref,
    lens_smem,
    first_kernel,
    first_bias,
    second_kernel,
    second_bias,
    gain,
    kext,
    w1,
    w2,
    rows32,
    x,
    ycat,
    second_out,
    embed_w,
    head_w,
    out_w,
    embedded,
    normed,
    queries,
    keys,
    vals,
    mixed,
    hide,
    load_sems,
    send_sems,
    recv_sems,
):
    inner = lax.axis_size("inner")
    devices = lax.axis_size("seq") * inner
    device = lax.axis_index("seq") * inner + lax.axis_index("inner")
    has_left = device > 0
    has_right = device < devices - 1
    right_id = lax.rem(device + 1, devices)
    left_id = lax.rem(device + devices - 1, devices)
    right = (right_id // inner, lax.rem(right_id, inner))
    left = (left_id // inner, lax.rem(left_id, inner))
    barrier = pltpu.get_barrier_semaphore()

    @pl.when(has_left)
    def greet_left():
        pl.semaphore_signal(barrier, inc=1, device_id=left, device_id_type=MESH)

    @pl.when(has_right)
    def greet_right():
        pl.semaphore_signal(barrier, inc=1, device_id=right, device_id_type=MESH)

    def load(source, target, index):
        copy = pltpu.make_async_copy(source, target, load_sems.at[index])
        copy.start()
        return copy

    def remote(source, target, index, neighbour):
        return pltpu.make_async_remote_copy(
            src_ref=source,
            dst_ref=target,
            send_sem=send_sems.at[index],
            recv_sem=recv_sems.at[index],
            device_id=neighbour,
            device_id_type=MESH,
        )

    small = [
        load(source, target, index)
        for index, (source, target) in enumerate(
            (
                (lens_hbm, lens_ref),
                (lens_hbm, lens_smem),
                (taps_hbm, first_kernel),
                (first_bias_hbm, first_bias),
                (second_hbm, second_kernel),
                (second_bias_hbm, second_bias),
                (gain_hbm, gain),
            )
        )
    ]
    load_raw = load(raw_hbm, raw, 7)
    cap = raw_hbm.shape[1]
    send_low = remote(raw_hbm.at[:, cap - SIDE : cap], low, 0, right)
    send_high = remote(raw_hbm.at[:, 0:SIDE], high, 1, left)
    send_tail = remote(
        normed.at[CTX + SHARD - SPAN : CTX + SHARD, :], normed.at[CTX - SPAN : CTX, :], 2, right
    )
    send_body = remote(
        normed.at[SHARD : CTX + SHARD - SPAN, :], normed.at[0 : CTX - SPAN, :], 3, right
    )
    send_head = remote(normed.at[CTX : CTX + SPAN, :], normed.at[CTX + SHARD :, :], 4, left)

    @pl.when(jnp.logical_not(has_left))
    def clear_left():
        low[...] = jnp.zeros_like(low)
        normed[0:CTX, :] = jnp.zeros((CTX, D), BF16)

    @pl.when(jnp.logical_not(has_right))
    def clear_right():
        high[...] = jnp.zeros_like(high)
        normed[CTX + SHARD :, :] = jnp.zeros((SPAN, D), BF16)

    for copy in small:
        copy.wait()
    base, starts = bounds(device, devices, lens_ref, lens_smem)
    build_taps(first_kernel, first_bias, kext)
    build_second(second_kernel, w2)
    build_hide(device, devices, base, starts, hide)
    spots = device * SHARD + lax.broadcasted_iota(jnp.int32, (SHARD, 1), 0)
    unused_seg, pos = locate(spots, base, starts)
    joined = pos > 0

    @pl.when(has_left & has_right)
    def meet_both():
        pl.semaphore_wait(barrier, 2)

    @pl.when(jnp.logical_not(has_left & has_right))
    def meet_one():
        pl.semaphore_wait(barrier, 1)

    @pl.when(has_right)
    def start_low():
        send_low.start()

    @pl.when(has_left)
    def start_high():
        send_high.start()

    load_embed = load(embed_hbm, embed_w, 8)
    load_head = load(head_hbm, head_w, 9)
    load_out = load(out_hbm, out_w, 10)
    build_first(kext, w1)
    load_raw.wait()
    rows32[0:256, :] = raw[:, 256:512].astype(F32).T
    build_inputs(128, CUT, MIDDLE, joined, rows32, x)
    convolve(0, MIDDLE, x, w1, w2, second_bias, ycat, second_out)

    @pl.when(has_right)
    def land_high():
        send_high.wait_recv()

    far = pick(device, base, starts, CTX, high, 2, raw[:, 512:768])
    rows32[...] = jnp.concatenate([raw[:, 384:512].astype(F32), far], axis=1).T
    build_inputs(128, CTX, CUT, joined, rows32, x)
    convolve(MIDDLE, CUT, x, w1, w2, second_bias, ycat, second_out)
    load_embed.wait()
    embed_rows(CUT, CTX, second_out, embed_w, embedded)
    norm_rows(CUT, CTX, embedded, gain, normed)

    @pl.when(has_right)
    def start_context():
        send_tail.start()
        send_body.start()

    @pl.when(has_left)
    def land_low():
        send_low.wait_recv()

    rows32[0:256, :] = pick(device, base, starts, -64, low, 0, raw[:, 128:384]).T
    build_inputs(64, 0, CUT, joined, rows32, x)
    convolve(0, CUT, x, w1, w2, second_bias, ycat, second_out)
    embed_rows(0, CUT, second_out, embed_w, embedded)
    norm_rows(0, CUT, embedded, gain, normed)

    @pl.when(has_left)
    def start_after():
        send_head.start()

    load_head.wait()
    queries[...] = head_rows(normed[CTX : CTX + SHARD, :], 0, head_w) * BF16(0.125)

    @pl.when(has_left)
    def land_tail():
        send_tail.wait_recv()

    for column, target in ((D, keys), (2 * D, vals)):
        target[CTX - SPAN : CTX + SHARD, :] = head_rows(
            normed[CTX - SPAN : CTX + SHARD, :], column, head_w
        )
    load_out.wait()
    shared = (queries, keys, vals, hide, mixed, embedded, out_w, encoded)
    attend_block(2, None, *shared)

    @pl.when(has_left)
    def land_body():
        send_body.wait_recv()

    @pl.when(has_right)
    def land_after():
        send_head.wait_recv()

    around = jnp.concatenate([normed[0 : CTX - SPAN, :], normed[CTX + SHARD :, :]], axis=0)
    for column, target in ((D, keys), (2 * D, vals)):
        result = head_rows(around, column, head_w)
        target[0 : CTX - SPAN, :] = result[: CTX - SPAN]
        target[CTX + SHARD :, :] = result[CTX - SPAN :]
    done = 2
    for block in (3, 1, 0):
        attend_block(block, done, *shared)
        done = block
    for piece in range(D // 256):
        project(done, piece, mixed, embedded, out_w, encoded)

    @pl.when(has_right)
    def sent_right():
        send_low.wait_send()
        send_tail.wait_send()
        send_body.wait_send()

    @pl.when(has_left)
    def sent_left():
        send_high.wait_send()
        send_head.wait_send()


def on_device(
    log_mel,
    lengths,
    first_kernel,
    first_bias,
    second_kernel,
    second_bias,
    embed_weight,
    norm_gain,
    head_weight,
    output_weight,
):
    hbm = pl.BlockSpec(memory_space=pltpu.HBM)
    return pl.pallas_call(
        layer_kernel,
        out_shape=jax.ShapeDtypeStruct((SHARD, D), BF16),
        in_specs=[hbm] * 10,
        out_specs=pl.BlockSpec(memory_space=pltpu.VMEM),
        scratch_shapes=[
            pltpu.VMEM((4 * MEL, log_mel.shape[0]), BF16),
            pltpu.VMEM((4 * MEL, SIDE), BF16),
            pltpu.VMEM((4 * MEL, SIDE), BF16),
            pltpu.VMEM(lengths.shape[::-1], jnp.int32),
            pltpu.SMEM(lengths.shape[::-1], jnp.int32),
            pltpu.VMEM((9, CH), BF16),
            pltpu.VMEM((1, CH), F32),
            pltpu.VMEM((9 * CH, CH), BF16),
            pltpu.VMEM((1, CH), F32),
            pltpu.VMEM((1, D), F32),
            pltpu.VMEM((32, 256), F32),
            pltpu.VMEM((256, BINS * 256), BF16),
            pltpu.VMEM((768, 256), BF16),
            pltpu.VMEM((2 * CUT, 4 * MEL), F32),
            pltpu.VMEM((3 * CUT, 256), BF16),
            pltpu.VMEM((2, CUT, 768), BF16),
            pltpu.VMEM((CTX, BINS * CH), BF16),
            pltpu.VMEM((BINS * CH, D), BF16),
            pltpu.VMEM((D, 3 * D), BF16),
            pltpu.VMEM((D, D), BF16),
            pltpu.VMEM((SHARD, D), BF16),
            pltpu.VMEM((KEY_ROWS, D), BF16),
            pltpu.VMEM((SHARD, D), BF16),
            pltpu.VMEM((KEY_ROWS, D), BF16),
            pltpu.VMEM((KEY_ROWS, D), BF16),
            pltpu.VMEM((SHARD, D), BF16),
            pltpu.VMEM((SHARD // QB, QB, QK), F32),
            pltpu.SemaphoreType.DMA((11,)),
            pltpu.SemaphoreType.DMA((5,)),
            pltpu.SemaphoreType.DMA((5,)),
        ],
        compiler_params=pltpu.CompilerParams(
            vmem_limit_bytes=48 * 2**20, collective_id=0, has_side_effects=True
        ),
        name="layer",
    )(
        *(
            pltpu.with_memory_space_constraint(value, pltpu.HBM)
            for value in (
                log_mel.T,
                lengths.T,
                first_kernel,
                first_bias.reshape(1, -1),
                second_kernel,
                second_bias.reshape(1, -1),
                norm_gain.reshape(1, -1),
                embed_weight,
                head_weight,
                output_weight,
            )
        )
    )


def solution(mesh):
    return jax.shard_map(
        on_device,
        mesh=mesh,
        in_specs=(P(AXES, None), P(), P(), P(), P(), P(), P(), P(), P(), P()),
        out_specs=P(AXES, None),
        check_vma=False,
    )
```

```python
import jax
import jax.numpy as jnp
from jax import lax
from jax.experimental import pallas as pl
from jax.experimental.pallas import tpu as pltpu
from jax.sharding import PartitionSpec as P

SPAN = 64
LEFT_SPANS = 4
CTX = 320
SHARD = 512
MARGIN = 192
MEL = 80
CH = 128
D = 1024
BINS = 20
CUT = 192
MIDDLE = 128
SIDE = 256
QB = 128
QK = 512
KEY_ROWS = CTX + SHARD + SPAN
AXES = ("seq", "inner")
F32 = jnp.float32
BF16 = jnp.bfloat16
MESH = pl.DeviceIdType.MESH


def bounds(device, devices, lens_ref, lens_smem):
    owners = lax.broadcasted_iota(jnp.int32, lens_ref.shape, 1)
    before = jnp.where(owners < device - 1, lens_ref[...].astype(F32), 0.0)
    base = jnp.sum(jnp.sum(before, axis=0, keepdims=True), axis=1, keepdims=True).astype(jnp.int32)
    starts = []
    total = jnp.int32(0)
    for step in (-1, 0, 1):
        owner = device + step
        real = (owner >= 0) & (owner < devices)
        safe = lax.rem(owner + devices, devices)
        for column in range(lens_smem.shape[0]):
            starts.append(total)
            total = total + jnp.where(real, lens_smem[column, safe], 0)
    return base, starts


def locate(spots, base, starts):
    rel = spots - base
    seg = jnp.zeros_like(rel)
    begin = jnp.zeros_like(rel)
    for start in starts[1:]:
        reached = rel >= start
        seg = seg + reached.astype(jnp.int32)
        begin = jnp.where(reached, start, begin)
    return seg, rel - begin


def codes(seg, pos):
    return seg * 64 + lax.shift_right_arithmetic(pos, 6)


def build_taps(first_kernel, first_bias, kext):
    kext[...] = jnp.zeros_like(kext)
    taps = first_kernel[...].astype(F32)
    for a in range(3):
        for b in range(3):
            row = taps[3 * a + b : 3 * a + b + 1, :]
            kext[5 * a + b : 5 * a + b + 1, 0:CH] = row
            kext[5 * a + b + 2 : 5 * a + b + 3, CH : 2 * CH] = row
    rest = first_bias[...]
    for part in range(3):
        piece = rest.astype(BF16).astype(F32)
        rest = rest - piece
        kext[15 + part : 16 + part, 0:CH] = piece
        kext[15 + part : 16 + part, CH : 2 * CH] = piece


def build_first(kext, w1):
    row = lax.broadcasted_iota(jnp.int32, (256, 32), 0)
    col = lax.broadcasted_iota(jnp.int32, (256, 32), 1)
    tap = (row >= MEL).astype(jnp.int32) + (row >= 2 * MEL).astype(jnp.int32)
    off = col - 5 * tap
    inside = (off >= 0) & (off <= 4) & (row < 3 * MEL)
    when = jnp.where(inside, row - MEL * tap + 1 - off, -1)
    always = jnp.where((row >= 3 * MEL) & (row - 3 * MEL + 15 == col), 1.0, 0.0)
    wide = kext[...].astype(BF16)
    for f in range(BINS):
        select = jnp.where(when == 4 * f, 1.0, always).astype(BF16)
        block = jnp.dot(select, wide, preferred_element_type=F32)
        w1[:, 256 * f : 256 * f + 256] = block.astype(BF16)


def build_second(second_kernel, w2):
    for a in range(3):
        base = 3 * a * CH
        w2[256 * a : 256 * a + 256, 0:CH] = second_kernel[base + CH : base + 3 * CH, :]
        w2[256 * a : 256 * a + CH, CH : 2 * CH] = jnp.zeros((CH, CH), BF16)
        w2[256 * a + CH : 256 * a + 256, CH : 2 * CH] = second_kernel[base : base + CH, :]


def pick(device, base, starts, first, far, owner_index, near):
    spots = device * SHARD + first + lax.broadcasted_iota(jnp.int32, (1, SIDE), 1)
    seg, unused_pos = locate(spots, base, starts)
    owner = lax.shift_right_arithmetic(seg, 2)
    return jnp.where(owner == owner_index, far[...].astype(F32), near.astype(F32))


def build_inputs(offset, begin, count, joined, rows32, x):
    here = joined[begin : begin + count]
    now = rows32[offset : offset + count, :]
    before = jnp.where(here, rows32[offset - 1 : offset + count - 1, :], 0.0)
    ones = jnp.ones((count, 16), F32)
    kept = jnp.where(here, ones, 0.0)
    x[0:count, :] = jnp.concatenate([before[:, MEL:], kept], axis=1).astype(BF16)
    x[count : 2 * count, :] = jnp.concatenate(
        [before[:, 3 * MEL :], now[:, : 2 * MEL], ones], axis=1
    ).astype(BF16)
    x[2 * count : 3 * count, :] = jnp.concatenate([now[:, MEL:], ones], axis=1).astype(BF16)


def convolve(begin, count, x, w1, w2, second_bias, ycat, second_out):
    bias = second_bias[...]
    lower = None
    for f in range(BINS):
        slot = f % 2
        y = jnp.dot(x[0 : 3 * count, :], w1[:, 256 * f : 256 * f + 256], preferred_element_type=F32)
        for a in range(3):
            ycat[slot, 0:count, 256 * a : 256 * a + 256] = jnp.maximum(
                y[a * count : (a + 1) * count], 0.0
            ).astype(BF16)
        r = jnp.dot(ycat[slot, 0:count, :], w2[...], preferred_element_type=F32)
        total = r[:, :CH] + bias if lower is None else r[:, :CH] + lower + bias
        lower = r[:, CH:]
        second_out[begin : begin + count, CH * f : CH * f + CH] = jnp.maximum(total, 0.0).astype(BF16)


def embed_rows(begin, count, second_out, embed_w, embedded):
    embedded[begin : begin + count, :] = jnp.dot(
        second_out[0:count, :], embed_w[...], preferred_element_type=F32
    ).astype(BF16)


def norm_rows(begin, count, embedded, gain, normed):
    for r in range(begin, begin + count, 64):
        values = embedded[r : r + 64, :].astype(F32)
        center = values - jnp.mean(values, axis=1, keepdims=True)
        spread = jnp.mean(center * center, axis=1, keepdims=True)
        normed[CTX + r : CTX + r + 64, :] = (
            center * lax.rsqrt(spread + 1e-05) * gain[...]
        ).astype(BF16)


def build_hide(device, devices, base, starts, hide):
    spots = device * SHARD - CTX + lax.broadcasted_iota(jnp.int32, (1, KEY_ROWS), 1)
    key_code = codes(*locate(spots, base, starts))
    key_code = jnp.where((spots >= 0) & (spots < devices * SHARD), key_code, -1000)
    for block in range(SHARD // QB):
        q_spots = device * SHARD + block * QB + lax.broadcasted_iota(jnp.int32, (QB, 1), 0)
        q_code = codes(*locate(q_spots, base, starts))
        gap = q_code - key_code[:, block * QB : block * QB + QK]
        hide[block] = jnp.where((gap >= 0) & (gap <= LEFT_SPANS), 0.0, -1e30)


def project(block, piece, mixed, embedded, out_w, encoded):
    rows = slice(block * QB, block * QB + QB)
    cols = slice(piece * 256, piece * 256 + 256)
    total = jnp.dot(mixed[rows, :], out_w[:, cols], preferred_element_type=F32)
    encoded[rows, cols] = (embedded[rows, cols].astype(F32) + total).astype(BF16)


def attend_block(block, done, queries, keys, vals, hide, mixed, embedded, out_w, encoded):
    rows = slice(block * QB, block * QB + QB)
    k_rows = slice(block * QB, block * QB + QK)
    left = lax.broadcasted_iota(jnp.int32, (QB, CH), 1) < 64
    ones = jnp.ones((QK, CH), BF16)
    for pair in range(D // CH):
        cols = slice(pair * CH, pair * CH + CH)
        q = queries[rows, cols]
        v = jnp.concatenate([vals[k_rows, cols], ones], axis=1)
        outs = []
        for half in (left, jnp.logical_not(left)):
            s = lax.dot_general(
                jnp.where(half, q, BF16(0)),
                keys[k_rows, cols],
                (((1,), (1,)), ((), ())),
                preferred_element_type=F32,
            )
            s = s + hide[block]
            p = jnp.exp(s - jnp.max(s, axis=1, keepdims=True)).astype(BF16)
            o = jnp.dot(p, v, preferred_element_type=F32)
            outs.append(o[:, :CH] / o[:, CH:])
        mixed[rows, cols] = jnp.where(left, outs[0], outs[1]).astype(BF16)
        if done is not None and pair % 2 == 1:
            project(done, pair // 2, mixed, embedded, out_w, encoded)


def head_rows(src, column, head_w):
    return jnp.dot(src, head_w[:, column : column + D], preferred_element_type=F32).astype(BF16)


def layer_kernel(
    raw_hbm,
    lens_hbm,
    taps_hbm,
    first_bias_hbm,
    second_hbm,
    second_bias_hbm,
    gain_hbm,
    embed_hbm,
    head_hbm,
    out_hbm,
    encoded,
    raw,
    low,
    high,
    lens_ref,
    lens_smem,
    first_kernel,
    first_bias,
    second_kernel,
    second_bias,
    gain,
    kext,
    w1,
    w2,
    rows32,
    x,
    ycat,
    second_out,
    embed_w,
    head_w,
    out_w,
    embedded,
    normed,
    queries,
    keys,
    vals,
    mixed,
    hide,
    load_sems,
    send_sems,
    recv_sems,
):
    inner = lax.axis_size("inner")
    devices = lax.axis_size("seq") * inner
    device = lax.axis_index("seq") * inner + lax.axis_index("inner")
    has_left = device > 0
    has_right = device < devices - 1
    right_id = lax.rem(device + 1, devices)
    left_id = lax.rem(device + devices - 1, devices)
    right = (right_id // inner, lax.rem(right_id, inner))
    left = (left_id // inner, lax.rem(left_id, inner))
    barrier = pltpu.get_barrier_semaphore()

    @pl.when(has_left)
    def greet_left():
        pl.semaphore_signal(barrier, inc=1, device_id=left, device_id_type=MESH)

    @pl.when(has_right)
    def greet_right():
        pl.semaphore_signal(barrier, inc=1, device_id=right, device_id_type=MESH)

    def load(source, target, index):
        copy = pltpu.make_async_copy(source, target, load_sems.at[index])
        copy.start()
        return copy

    def remote(source, target, index, neighbour):
        return pltpu.make_async_remote_copy(
            src_ref=source,
            dst_ref=target,
            send_sem=send_sems.at[index],
            recv_sem=recv_sems.at[index],
            device_id=neighbour,
            device_id_type=MESH,
        )

    small = [
        load(source, target, index)
        for index, (source, target) in enumerate(
            (
                (lens_hbm, lens_ref),
                (lens_hbm, lens_smem),
                (taps_hbm, first_kernel),
                (first_bias_hbm, first_bias),
                (second_hbm, second_kernel),
                (second_bias_hbm, second_bias),
                (gain_hbm, gain),
            )
        )
    ]
    load_raw = load(raw_hbm, raw, 7)
    cap = raw_hbm.shape[1]
    send_low = remote(raw.at[:, cap - SIDE : cap], low, 0, right)
    send_high = remote(raw.at[:, 0:SIDE], high, 1, left)
    send_tail = remote(
        normed.at[CTX + SHARD - SPAN : CTX + SHARD, :], normed.at[CTX - SPAN : CTX, :], 2, right
    )
    send_body = remote(
        normed.at[2 * CTX : CTX + SHARD - SPAN, :], normed.at[MIDDLE : CTX - SPAN, :], 3, right
    )
    send_middle = remote(normed.at[SHARD : 2 * CTX, :], normed.at[0:MIDDLE, :], 5, right)
    send_head = remote(normed.at[CTX : CTX + SPAN, :], normed.at[CTX + SHARD :, :], 4, left)

    @pl.when(jnp.logical_not(has_left))
    def clear_left():
        low[...] = jnp.zeros_like(low)
        normed[0:CTX, :] = jnp.zeros((CTX, D), BF16)

    @pl.when(jnp.logical_not(has_right))
    def clear_right():
        high[...] = jnp.zeros_like(high)
        normed[CTX + SHARD :, :] = jnp.zeros((SPAN, D), BF16)

    for copy in small:
        copy.wait()
    base, starts = bounds(device, devices, lens_ref, lens_smem)
    build_taps(first_kernel, first_bias, kext)
    build_second(second_kernel, w2)
    build_hide(device, devices, base, starts, hide)
    spots = device * SHARD + lax.broadcasted_iota(jnp.int32, (SHARD, 1), 0)
    unused_seg, pos = locate(spots, base, starts)
    joined = pos > 0

    load_raw.wait()

    @pl.when(has_left & has_right)
    def meet_both():
        pl.semaphore_wait(barrier, 2)

    @pl.when(jnp.logical_not(has_left & has_right))
    def meet_one():
        pl.semaphore_wait(barrier, 1)

    @pl.when(has_right)
    def start_low():
        send_low.start()

    @pl.when(has_left)
    def start_high():
        send_high.start()

    load_embed = load(embed_hbm, embed_w, 8)
    load_head = load(head_hbm, head_w, 9)
    load_out = load(out_hbm, out_w, 10)
    build_first(kext, w1)
    rows32[0:256, :] = raw[:, 256:512].astype(F32).T
    build_inputs(128, CUT, MIDDLE, joined, rows32, x)
    convolve(0, MIDDLE, x, w1, w2, second_bias, ycat, second_out)

    load_embed.wait()
    embed_rows(CUT, MIDDLE, second_out, embed_w, embedded)
    norm_rows(CUT, MIDDLE, embedded, gain, normed)

    @pl.when(has_right)
    def start_middle():
        send_middle.start()

    @pl.when(has_right)
    def land_high():
        send_high.wait_recv()

    far = pick(device, base, starts, CTX, high, 2, raw[:, 512:768])
    rows32[...] = jnp.concatenate([raw[:, 384:512].astype(F32), far], axis=1).T
    build_inputs(128, CTX, CUT, joined, rows32, x)
    convolve(0, CUT, x, w1, w2, second_bias, ycat, second_out)
    embed_rows(CTX, CUT, second_out, embed_w, embedded)
    norm_rows(CTX, CUT, embedded, gain, normed)

    @pl.when(has_right)
    def start_context():
        send_tail.start()
        send_body.start()

    @pl.when(has_left)
    def land_low():
        send_low.wait_recv()

    rows32[0:256, :] = pick(device, base, starts, -64, low, 0, raw[:, 128:384]).T
    build_inputs(64, 0, CUT, joined, rows32, x)
    convolve(0, CUT, x, w1, w2, second_bias, ycat, second_out)
    embed_rows(0, CUT, second_out, embed_w, embedded)
    norm_rows(0, CUT, embedded, gain, normed)

    @pl.when(has_left)
    def start_after():
        send_head.start()

    load_head.wait()
    queries[...] = head_rows(normed[CTX : CTX + SHARD, :], 0, head_w) * BF16(0.125)

    @pl.when(has_left)
    def land_tail():
        send_tail.wait_recv()

    for column, target in ((D, keys), (2 * D, vals)):
        target[CTX - SPAN : CTX + SHARD, :] = head_rows(
            normed[CTX - SPAN : CTX + SHARD, :], column, head_w
        )
    load_out.wait()
    shared = (queries, keys, vals, hide, mixed, embedded, out_w, encoded)
    attend_block(2, None, *shared)

    @pl.when(has_left)
    def land_body():
        send_middle.wait_recv()
        send_body.wait_recv()

    @pl.when(has_right)
    def land_after():
        send_head.wait_recv()

    around = jnp.concatenate([normed[0 : CTX - SPAN, :], normed[CTX + SHARD :, :]], axis=0)
    for column, target in ((D, keys), (2 * D, vals)):
        result = head_rows(around, column, head_w)
        target[0 : CTX - SPAN, :] = result[: CTX - SPAN]
        target[CTX + SHARD :, :] = result[CTX - SPAN :]
    done = 2
    for block in (3, 1, 0):
        attend_block(block, done, *shared)
        done = block
    for piece in range(D // 256):
        project(done, piece, mixed, embedded, out_w, encoded)

    @pl.when(has_right)
    def sent_right():
        send_low.wait_send()
        send_tail.wait_send()
        send_middle.wait_send()
        send_body.wait_send()

    @pl.when(has_left)
    def sent_left():
        send_high.wait_send()
        send_head.wait_send()


def on_device(
    log_mel,
    lengths,
    first_kernel,
    first_bias,
    second_kernel,
    second_bias,
    embed_weight,
    norm_gain,
    head_weight,
    output_weight,
):
    hbm = pl.BlockSpec(memory_space=pltpu.HBM)
    return pl.pallas_call(
        layer_kernel,
        out_shape=jax.ShapeDtypeStruct((SHARD, D), BF16),
        in_specs=[hbm] * 10,
        out_specs=pl.BlockSpec(memory_space=pltpu.VMEM),
        scratch_shapes=[
            pltpu.VMEM((4 * MEL, log_mel.shape[0]), BF16),
            pltpu.VMEM((4 * MEL, SIDE), BF16),
            pltpu.VMEM((4 * MEL, SIDE), BF16),
            pltpu.VMEM(lengths.shape[::-1], jnp.int32),
            pltpu.SMEM(lengths.shape[::-1], jnp.int32),
            pltpu.VMEM((9, CH), BF16),
            pltpu.VMEM((1, CH), F32),
            pltpu.VMEM((9 * CH, CH), BF16),
            pltpu.VMEM((1, CH), F32),
            pltpu.VMEM((1, D), F32),
            pltpu.VMEM((32, 256), F32),
            pltpu.VMEM((256, BINS * 256), BF16),
            pltpu.VMEM((768, 256), BF16),
            pltpu.VMEM((2 * CUT, 4 * MEL), F32),
            pltpu.VMEM((3 * CUT, 256), BF16),
            pltpu.VMEM((2, CUT, 768), BF16),
            pltpu.VMEM((CUT, BINS * CH), BF16),
            pltpu.VMEM((BINS * CH, D), BF16),
            pltpu.VMEM((D, 3 * D), BF16),
            pltpu.VMEM((D, D), BF16),
            pltpu.VMEM((SHARD, D), BF16),
            pltpu.VMEM((KEY_ROWS, D), BF16),
            pltpu.VMEM((SHARD, D), BF16),
            pltpu.VMEM((KEY_ROWS, D), BF16),
            pltpu.VMEM((KEY_ROWS, D), BF16),
            pltpu.VMEM((SHARD, D), BF16),
            pltpu.VMEM((SHARD // QB, QB, QK), F32),
            pltpu.SemaphoreType.DMA((11,)),
            pltpu.SemaphoreType.DMA((6,)),
            pltpu.SemaphoreType.DMA((6,)),
        ],
        compiler_params=pltpu.CompilerParams(
            vmem_limit_bytes=48 * 2**20, collective_id=0, has_side_effects=True
        ),
        name="layer",
    )(
        *(
            pltpu.with_memory_space_constraint(value, pltpu.HBM)
            for value in (
                log_mel.T,
                lengths.T,
                first_kernel,
                first_bias.reshape(1, -1),
                second_kernel,
                second_bias.reshape(1, -1),
                norm_gain.reshape(1, -1),
                embed_weight,
                head_weight,
                output_weight,
            )
        )
    )


def solution(mesh):
    return jax.shard_map(
        on_device,
        mesh=mesh,
        in_specs=(P(AXES, None), P(), P(), P(), P(), P(), P(), P(), P(), P()),
        out_specs=P(AXES, None),
        check_vma=False,
    )
```

```python
import jax
import jax.numpy as jnp
from jax import lax
from jax.experimental import pallas as pl
from jax.experimental.pallas import tpu as pltpu
from jax.sharding import PartitionSpec as P

SPAN = 64
LEFT_SPANS = 4
CTX = 320
SHARD = 512
MARGIN = 192
MEL = 80
CH = 128
D = 1024
BINS = 20
CUT = 192
MIDDLE = 128
SIDE = 256
QB = 128
QK = 512
KEY_ROWS = CTX + SHARD + SPAN
AXES = ("seq", "inner")
F32 = jnp.float32
BF16 = jnp.bfloat16
MESH = pl.DeviceIdType.MESH


def bounds(device, devices, lens_ref, lens_smem):
    owners = lax.broadcasted_iota(jnp.int32, lens_ref.shape, 1)
    before = jnp.where(owners < device - 1, lens_ref[...].astype(F32), 0.0)
    base = jnp.sum(jnp.sum(before, axis=0, keepdims=True), axis=1, keepdims=True).astype(jnp.int32)
    starts = []
    total = jnp.int32(0)
    for step in (-1, 0, 1):
        owner = device + step
        real = (owner >= 0) & (owner < devices)
        safe = lax.rem(owner + devices, devices)
        for column in range(lens_smem.shape[0]):
            starts.append(total)
            total = total + jnp.where(real, lens_smem[column, safe], 0)
    return base, starts


def locate(spots, base, starts):
    rel = spots - base
    seg = jnp.zeros_like(rel)
    begin = jnp.zeros_like(rel)
    for start in starts[1:]:
        reached = rel >= start
        seg = seg + reached.astype(jnp.int32)
        begin = jnp.where(reached, start, begin)
    return seg, rel - begin


def codes(seg, pos):
    return seg * 64 + lax.shift_right_arithmetic(pos, 6)


def build_taps(first_kernel, first_bias, kext):
    kext[...] = jnp.zeros_like(kext)
    taps = first_kernel[...].astype(F32)
    for a in range(3):
        for b in range(3):
            row = taps[3 * a + b : 3 * a + b + 1, :]
            kext[5 * a + b : 5 * a + b + 1, 0:CH] = row
            kext[5 * a + b + 2 : 5 * a + b + 3, CH : 2 * CH] = row
    rest = first_bias[...]
    for part in range(3):
        piece = rest.astype(BF16).astype(F32)
        rest = rest - piece
        kext[15 + part : 16 + part, 0:CH] = piece
        kext[15 + part : 16 + part, CH : 2 * CH] = piece


def build_first(kext, w1):
    row = lax.broadcasted_iota(jnp.int32, (256, 32), 0)
    col = lax.broadcasted_iota(jnp.int32, (256, 32), 1)
    tap = (row >= MEL).astype(jnp.int32) + (row >= 2 * MEL).astype(jnp.int32)
    off = col - 5 * tap
    inside = (off >= 0) & (off <= 4) & (row < 3 * MEL)
    when = jnp.where(inside, row - MEL * tap + 1 - off, -1)
    always = jnp.where((row >= 3 * MEL) & (row - 3 * MEL + 15 == col), 1.0, 0.0)
    wide = kext[...].astype(BF16)
    for f in range(BINS):
        select = jnp.where(when == 4 * f, 1.0, always).astype(BF16)
        block = jnp.dot(select, wide, preferred_element_type=F32)
        w1[:, 256 * f : 256 * f + 256] = block.astype(BF16)


def build_second(second_kernel, w2):
    for a in range(3):
        base = 3 * a * CH
        w2[256 * a : 256 * a + 256, 0:CH] = second_kernel[base + CH : base + 3 * CH, :]
        w2[256 * a : 256 * a + CH, CH : 2 * CH] = jnp.zeros((CH, CH), BF16)
        w2[256 * a + CH : 256 * a + 256, CH : 2 * CH] = second_kernel[base : base + CH, :]


def pick(device, base, starts, first, far, owner_index, near):
    spots = device * SHARD + first + lax.broadcasted_iota(jnp.int32, (1, SIDE), 1)
    seg, unused_pos = locate(spots, base, starts)
    owner = lax.shift_right_arithmetic(seg, 2)
    return jnp.where(owner == owner_index, far[...].astype(F32), near.astype(F32))


def build_inputs(offset, begin, count, joined, rows32, x):
    here = joined[begin : begin + count]
    now = rows32[offset : offset + count, :]
    before = jnp.where(here, rows32[offset - 1 : offset + count - 1, :], 0.0)
    ones = jnp.ones((count, 16), F32)
    kept = jnp.where(here, ones, 0.0)
    x[0:count, :] = jnp.concatenate([before[:, MEL:], kept], axis=1).astype(BF16)
    x[count : 2 * count, :] = jnp.concatenate(
        [before[:, 3 * MEL :], now[:, : 2 * MEL], ones], axis=1
    ).astype(BF16)
    x[2 * count : 3 * count, :] = jnp.concatenate([now[:, MEL:], ones], axis=1).astype(BF16)


def convolve(begin, count, x, w1, w2, second_bias, ycat, second_out):
    bias = second_bias[...]
    lower = None
    for f in range(BINS):
        slot = f % 2
        y = jnp.dot(x[0 : 3 * count, :], w1[:, 256 * f : 256 * f + 256], preferred_element_type=F32)
        for a in range(3):
            ycat[slot, 0:count, 256 * a : 256 * a + 256] = jnp.maximum(
                y[a * count : (a + 1) * count], 0.0
            ).astype(BF16)
        r = jnp.dot(ycat[slot, 0:count, :], w2[...], preferred_element_type=F32)
        total = r[:, :CH] + bias if lower is None else r[:, :CH] + lower + bias
        lower = r[:, CH:]
        second_out[begin : begin + count, CH * f : CH * f + CH] = jnp.maximum(total, 0.0).astype(BF16)


def embed_rows(begin, count, second_out, embed_w, embedded):
    embedded[begin : begin + count, :] = jnp.dot(
        second_out[0:count, :], embed_w[...], preferred_element_type=F32
    ).astype(BF16)


def norm_rows(begin, count, embedded, gain, normed):
    for r in range(begin, begin + count, 64):
        values = embedded[r : r + 64, :].astype(F32)
        center = values - jnp.mean(values, axis=1, keepdims=True)
        spread = jnp.mean(center * center, axis=1, keepdims=True)
        normed[CTX + r : CTX + r + 64, :] = (
            center * lax.rsqrt(spread + 1e-05) * gain[...]
        ).astype(BF16)


def build_hide(device, devices, base, starts, query_code, hide):
    spots = device * SHARD - CTX + lax.broadcasted_iota(jnp.int32, (1, KEY_ROWS), 1)
    key_code = codes(*locate(spots, base, starts))
    key_code = jnp.where((spots >= 0) & (spots < devices * SHARD), key_code, -1000)
    for block in range(SHARD // QB):
        q_code = query_code[block * QB : block * QB + QB]
        gap = q_code - key_code[:, block * QB : block * QB + QK]
        hide[block] = jnp.where((gap >= 0) & (gap <= LEFT_SPANS), 0.0, -1e30)


def project(block, piece, mixed, embedded, out_w, encoded):
    rows = slice(block * QB, block * QB + QB)
    cols = slice(piece * 256, piece * 256 + 256)
    total = jnp.dot(mixed[rows, :], out_w[:, cols], preferred_element_type=F32)
    encoded[rows, cols] = (embedded[rows, cols].astype(F32) + total).astype(BF16)


def attend_block(block, done, queries, keys, vals, hide, mixed, embedded, out_w, encoded):
    rows = slice(block * QB, block * QB + QB)
    k_rows = slice(block * QB, block * QB + QK)
    left = lax.broadcasted_iota(jnp.int32, (QB, CH), 1) < 64
    ones = jnp.ones((QK, CH), BF16)
    for pair in range(D // CH):
        cols = slice(pair * CH, pair * CH + CH)
        q = queries[rows, cols]
        v = jnp.concatenate([vals[k_rows, cols], ones], axis=1)
        outs = []
        for half in (left, jnp.logical_not(left)):
            s = lax.dot_general(
                jnp.where(half, q, BF16(0)),
                keys[k_rows, cols],
                (((1,), (1,)), ((), ())),
                preferred_element_type=F32,
            )
            s = s + hide[block]
            p = jnp.exp(s - jnp.max(s, axis=1, keepdims=True)).astype(BF16)
            o = jnp.dot(p, v, preferred_element_type=F32)
            outs.append(o[:, :CH] / o[:, CH:])
        mixed[rows, cols] = jnp.where(left, outs[0], outs[1]).astype(BF16)
        if done is not None and pair % 2 == 1:
            project(done, pair // 2, mixed, embedded, out_w, encoded)


def head_rows(src, column, head_w):
    return jnp.dot(src, head_w[:, column : column + D], preferred_element_type=F32).astype(BF16)


def layer_kernel(
    raw_hbm,
    lens_hbm,
    taps_hbm,
    first_bias_hbm,
    second_hbm,
    second_bias_hbm,
    gain_hbm,
    embed_hbm,
    head_hbm,
    out_hbm,
    encoded,
    raw,
    low,
    high,
    lens_ref,
    lens_smem,
    first_kernel,
    first_bias,
    second_kernel,
    second_bias,
    gain,
    kext,
    w1,
    w2,
    rows32,
    x,
    ycat,
    second_out,
    embed_w,
    head_w,
    out_w,
    embedded,
    normed,
    queries,
    keys,
    vals,
    mixed,
    hide,
    load_sems,
    send_sems,
    recv_sems,
):
    inner = lax.axis_size("inner")
    devices = lax.axis_size("seq") * inner
    device = lax.axis_index("seq") * inner + lax.axis_index("inner")
    has_left = device > 0
    has_right = device < devices - 1
    right_id = lax.rem(device + 1, devices)
    left_id = lax.rem(device + devices - 1, devices)
    right = (right_id // inner, lax.rem(right_id, inner))
    left = (left_id // inner, lax.rem(left_id, inner))
    barrier = pltpu.get_barrier_semaphore()

    @pl.when(has_left)
    def greet_left():
        pl.semaphore_signal(barrier, inc=1, device_id=left, device_id_type=MESH)

    @pl.when(has_right)
    def greet_right():
        pl.semaphore_signal(barrier, inc=1, device_id=right, device_id_type=MESH)

    def load(source, target, index):
        copy = pltpu.make_async_copy(source, target, load_sems.at[index])
        copy.start()
        return copy

    def remote(source, target, index, neighbour):
        return pltpu.make_async_remote_copy(
            src_ref=source,
            dst_ref=target,
            send_sem=send_sems.at[index],
            recv_sem=recv_sems.at[index],
            device_id=neighbour,
            device_id_type=MESH,
        )

    small = [
        load(source, target, index)
        for index, (source, target) in enumerate(
            (
                (lens_hbm, lens_ref),
                (lens_hbm, lens_smem),
                (taps_hbm, first_kernel),
                (first_bias_hbm, first_bias),
                (second_hbm, second_kernel),
                (second_bias_hbm, second_bias),
                (gain_hbm, gain),
            )
        )
    ]
    load_raw = load(raw_hbm, raw, 7)
    cap = raw_hbm.shape[1]
    send_low = remote(raw.at[:, cap - SIDE : cap], low, 0, right)
    send_high = remote(raw.at[:, 0:SIDE], high, 1, left)
    send_tail = remote(
        normed.at[CTX + SHARD - SPAN : CTX + SHARD, :], normed.at[CTX - SPAN : CTX, :], 2, right
    )
    send_body = remote(
        normed.at[2 * CTX : CTX + SHARD - SPAN, :], normed.at[MIDDLE : CTX - SPAN, :], 3, right
    )
    send_middle = remote(normed.at[SHARD : 2 * CTX, :], normed.at[0:MIDDLE, :], 5, right)
    send_head = remote(normed.at[CTX : CTX + SPAN, :], normed.at[CTX + SHARD :, :], 4, left)

    @pl.when(jnp.logical_not(has_left))
    def clear_left():
        low[...] = jnp.zeros_like(low)
        normed[0:CTX, :] = jnp.zeros((CTX, D), BF16)

    @pl.when(jnp.logical_not(has_right))
    def clear_right():
        high[...] = jnp.zeros_like(high)
        normed[CTX + SHARD :, :] = jnp.zeros((SPAN, D), BF16)

    for copy in small:
        copy.wait()
    base, starts = bounds(device, devices, lens_ref, lens_smem)
    build_taps(first_kernel, first_bias, kext)
    build_second(second_kernel, w2)
    spots = device * SHARD + lax.broadcasted_iota(jnp.int32, (SHARD, 1), 0)
    seg, pos = locate(spots, base, starts)
    joined = pos > 0
    build_hide(device, devices, base, starts, codes(seg, pos), hide)

    load_raw.wait()

    @pl.when(has_left & has_right)
    def meet_both():
        pl.semaphore_wait(barrier, 2)

    @pl.when(jnp.logical_not(has_left & has_right))
    def meet_one():
        pl.semaphore_wait(barrier, 1)

    @pl.when(has_right)
    def start_low():
        send_low.start()

    @pl.when(has_left)
    def start_high():
        send_high.start()

    load_embed = load(embed_hbm, embed_w, 8)
    load_head = load(head_hbm, head_w, 9)
    load_out = load(out_hbm, out_w, 10)
    build_first(kext, w1)
    rows32[0:256, :] = raw[:, 256:512].astype(F32).T
    build_inputs(128, CUT, MIDDLE, joined, rows32, x)
    convolve(0, MIDDLE, x, w1, w2, second_bias, ycat, second_out)

    load_embed.wait()
    embed_rows(CUT, MIDDLE, second_out, embed_w, embedded)
    norm_rows(CUT, MIDDLE, embedded, gain, normed)

    @pl.when(has_right)
    def start_middle():
        send_middle.start()

    @pl.when(has_right)
    def land_high():
        send_high.wait_recv()

    far = pick(device, base, starts, CTX, high, 2, raw[:, 512:768])
    rows32[...] = jnp.concatenate([raw[:, 384:512].astype(F32), far], axis=1).T
    build_inputs(128, CTX, CUT, joined, rows32, x)
    convolve(0, CUT, x, w1, w2, second_bias, ycat, second_out)
    embed_rows(CTX, CUT, second_out, embed_w, embedded)
    norm_rows(CTX, CUT, embedded, gain, normed)

    @pl.when(has_right)
    def start_context():
        send_tail.start()
        send_body.start()

    @pl.when(has_left)
    def land_low():
        send_low.wait_recv()

    rows32[0:256, :] = pick(device, base, starts, -64, low, 0, raw[:, 128:384]).T
    build_inputs(64, 0, CUT, joined, rows32, x)
    convolve(0, CUT, x, w1, w2, second_bias, ycat, second_out)
    embed_rows(0, CUT, second_out, embed_w, embedded)
    norm_rows(0, CUT, embedded, gain, normed)

    @pl.when(has_left)
    def start_after():
        send_head.start()

    load_head.wait()
    queries[...] = head_rows(normed[CTX : CTX + SHARD, :], 0, head_w) * BF16(0.125)

    @pl.when(has_left)
    def land_tail():
        send_tail.wait_recv()

    for column, target in ((D, keys), (2 * D, vals)):
        target[CTX - SPAN : CTX + SHARD, :] = head_rows(
            normed[CTX - SPAN : CTX + SHARD, :], column, head_w
        )
    load_out.wait()
    shared = (queries, keys, vals, hide, mixed, embedded, out_w, encoded)
    attend_block(2, None, *shared)

    @pl.when(has_left)
    def land_body():
        send_middle.wait_recv()
        send_body.wait_recv()

    @pl.when(has_right)
    def land_after():
        send_head.wait_recv()

    around = jnp.concatenate([normed[0 : CTX - SPAN, :], normed[CTX + SHARD :, :]], axis=0)
    for column, target in ((D, keys), (2 * D, vals)):
        result = head_rows(around, column, head_w)
        target[0 : CTX - SPAN, :] = result[: CTX - SPAN]
        target[CTX + SHARD :, :] = result[CTX - SPAN :]
    done = 2
    for block in (3, 1, 0):
        attend_block(block, done, *shared)
        done = block
    for piece in range(D // 256):
        project(done, piece, mixed, embedded, out_w, encoded)

    @pl.when(has_right)
    def sent_right():
        send_low.wait_send()
        send_tail.wait_send()
        send_middle.wait_send()
        send_body.wait_send()

    @pl.when(has_left)
    def sent_left():
        send_high.wait_send()
        send_head.wait_send()


def on_device(
    log_mel,
    lengths,
    first_kernel,
    first_bias,
    second_kernel,
    second_bias,
    embed_weight,
    norm_gain,
    head_weight,
    output_weight,
):
    hbm = pl.BlockSpec(memory_space=pltpu.HBM)
    return pl.pallas_call(
        layer_kernel,
        out_shape=jax.ShapeDtypeStruct((SHARD, D), BF16),
        in_specs=[hbm] * 10,
        out_specs=pl.BlockSpec(memory_space=pltpu.VMEM),
        scratch_shapes=[
            pltpu.VMEM((4 * MEL, log_mel.shape[0]), BF16),
            pltpu.VMEM((4 * MEL, SIDE), BF16),
            pltpu.VMEM((4 * MEL, SIDE), BF16),
            pltpu.VMEM(lengths.shape[::-1], jnp.int32),
            pltpu.SMEM(lengths.shape[::-1], jnp.int32),
            pltpu.VMEM((9, CH), BF16),
            pltpu.VMEM((1, CH), F32),
            pltpu.VMEM((9 * CH, CH), BF16),
            pltpu.VMEM((1, CH), F32),
            pltpu.VMEM((1, D), F32),
            pltpu.VMEM((32, 256), F32),
            pltpu.VMEM((256, BINS * 256), BF16),
            pltpu.VMEM((768, 256), BF16),
            pltpu.VMEM((2 * CUT, 4 * MEL), F32),
            pltpu.VMEM((3 * CUT, 256), BF16),
            pltpu.VMEM((2, CUT, 768), BF16),
            pltpu.VMEM((CUT, BINS * CH), BF16),
            pltpu.VMEM((BINS * CH, D), BF16),
            pltpu.VMEM((D, 3 * D), BF16),
            pltpu.VMEM((D, D), BF16),
            pltpu.VMEM((SHARD, D), BF16),
            pltpu.VMEM((KEY_ROWS, D), BF16),
            pltpu.VMEM((SHARD, D), BF16),
            pltpu.VMEM((KEY_ROWS, D), BF16),
            pltpu.VMEM((KEY_ROWS, D), BF16),
            pltpu.VMEM((SHARD, D), BF16),
            pltpu.VMEM((SHARD // QB, QB, QK), F32),
            pltpu.SemaphoreType.DMA((11,)),
            pltpu.SemaphoreType.DMA((6,)),
            pltpu.SemaphoreType.DMA((6,)),
        ],
        compiler_params=pltpu.CompilerParams(
            vmem_limit_bytes=48 * 2**20, collective_id=0, has_side_effects=True
        ),
        name="layer",
    )(
        *(
            pltpu.with_memory_space_constraint(value, pltpu.HBM)
            for value in (
                log_mel.T,
                lengths.T,
                first_kernel,
                first_bias.reshape(1, -1),
                second_kernel,
                second_bias.reshape(1, -1),
                norm_gain.reshape(1, -1),
                embed_weight,
                head_weight,
                output_weight,
            )
        )
    )


def solution(mesh):
    return jax.shard_map(
        on_device,
        mesh=mesh,
        in_specs=(P(AXES, None), P(), P(), P(), P(), P(), P(), P(), P(), P()),
        out_specs=P(AXES, None),
        check_vma=False,
    )
```
